32 devices in a mesh: groups: 2 (over y), dp: 2 (over core), seq: 8 (over z, x).
Axes of the slice: x: 2, y: 2, z: 4, core: 2. Of those that a mesh axis runs over, the one named last changes fastest.
Arguments:
- query_proj: bfloat16 [4, 1024, 2048], P(('groups', 'dp'), 'seq'), parts along dimension 0, may hold values from -6 to 6
- key_proj: bfloat16 [4, 1024, 2048], P(('groups', 'dp'), 'seq'), parts along dimension 0, may hold values from -6 to 6
- value_proj: bfloat16 [4, 1024, 2048], P(('groups', 'dp'), 'seq'), parts along dimension 0, may hold values from -6 to 6
- cotangent: bfloat16 [4, 1024, 2048], P(('groups', 'dp'), 'seq'), parts along dimension 0, may hold values from -6 to 6
- boundary: int32 [4], P(('groups', 'dp')), parts along dimension 0, may hold values from 128 to 511
- short_taps: float32 [3, 3, 2048], replicated, may hold values from -3 to 3
- skip_gain: float32 [2048], replicated, may hold values from -4 to 4
- long_filter: bfloat16 [1024, 2048], P('seq'), may hold values from -1.1 to 1.1
Outputs:
- query_grad: bfloat16 [4, 1024, 2048], P(('groups', 'dp'), 'seq'), parts along dimension 0
- key_grad: bfloat16 [4, 1024, 2048], P(('groups', 'dp'), 'seq'), parts along dimension 0
- value_grad: bfloat16 [4, 1024, 2048], P(('groups', 'dp'), 'seq'), parts along dimension 0
- filter_grad: bfloat16 [2048, 2048], P(('groups', 'seq')), parts along dimension 0
- taps_grad: float32 [6, 3, 2048], P('groups', None, 'seq'), parts along dimension 0
- skip_grad: float32 [4096], P(('groups', 'seq')), parts along dimension 0
The draws below stay inside these ranges and needn't reach their ends.
There are 2 independent parts, one for each index of `groups`. The reference program is written for one: setup_inputs(seed, part) draws one part's arguments, and reference() takes and returns one part's arrays. A program takes and returns all parts, laid end to end along the dimension named above; an argument that names none is the same for every part. Nothing has to cross between parts.
All inputs are finite; a program needn't handle non-finite values.
Results may differ from the reference program's by a relative error of at most 0.001.
Values may be sent and summed in bfloat16 or wider, within the bound.
A program may use at most 128 MiB of HBM per device.

```python
import math
import jax
import jax.numpy as jnp
from jax import lax

CH = 2048
PAIRS = 2
SEQ_LEN = 1024


def draw_long_filter(key, part):
    key_noise = jax.random.fold_in(key, 11)
    key_rate = jax.random.fold_in(key, 12)
    key_kind = jax.random.fold_in(key, 13)
    steps = jnp.arange(SEQ_LEN, dtype=jnp.float32)[:, None]
    spread = jax.random.uniform(key_rate, (1, CH), dtype=jnp.float32)
    noise = jnp.clip(jax.random.normal(key_noise, (SEQ_LEN, CH), dtype=jnp.float32), -4.0, 4.0)
    slow = (jax.random.uniform(key_kind, (1, CH), dtype=jnp.float32) < 0.5).astype(jnp.float32)
    slow_rate = (0.2 + 1.8 * spread) / SEQ_LEN
    fast_rate = 1.0 / (30.0 + 20.0 * spread)
    rate = jnp.minimum(slow * slow_rate + (1.0 - slow) * fast_rate, 1.0 / 30.0)
    return (noise * jnp.sqrt(2.0 * rate) * jnp.exp(-rate * steps)).astype(jnp.bfloat16)


def shard_levels(key, shape, pieces, smallest, high):
    def one(position, blocks):
        heights = jax.random.uniform(jax.random.fold_in(jax.random.fold_in(key, 6), position), (blocks,), jnp.float32, smallest / len(pieces), high / len(pieces))
        return jnp.repeat(jnp.exp(heights), shape[position] // blocks).reshape((-1,) + (1,) * (len(shape) - position - 1))

    gain = one(*pieces[0])
    for cut in pieces[1:]:
        gain = gain * one(*cut)
    return gain


def gaussian(rng, dims, scale, bound, cuts=(), held_as=jnp.bfloat16):
    drawn = scale * jax.random.normal(rng, dims, jnp.float32)
    if cuts:
        drawn = drawn * shard_levels(rng, dims, cuts, -0.22, 0.18)
    return jnp.clip(drawn, -bound, bound).astype(held_as)


def setup_inputs(seed: int = 0, part: int = 0) -> dict:
    arg_keys = jax.random.split(jax.random.key(seed), 9)
    part_splits = jax.random.split(jax.random.fold_in(arg_keys[8], part), 9)
    return {
        "query_proj": gaussian(part_splits[0], (PAIRS, SEQ_LEN, CH), 1.0, 6.0, ((0, 2), (1, 8))),
        "key_proj": gaussian(part_splits[1], (PAIRS, SEQ_LEN, CH), 1.0, 6.0, ((0, 2), (1, 8))),
        "value_proj": gaussian(part_splits[2], (PAIRS, SEQ_LEN, CH), 1.0, 6.0, ((0, 2), (1, 8))),
        "cotangent": gaussian(part_splits[3], (PAIRS, SEQ_LEN, CH), 1.0, 6.0, ((0, 2), (1, 8))),
        "boundary": jax.random.randint(part_splits[4], (PAIRS,), SEQ_LEN // 8, SEQ_LEN // 2).astype(jnp.int32),
        "short_taps": gaussian(arg_keys[5], (3, 3, CH), 0.6, 3.0, (), jnp.float32),
        "skip_gain": gaussian(arg_keys[6], (CH,), 1.0, 4.0, (), jnp.float32),
        "long_filter": draw_long_filter(jax.random.fold_in(arg_keys[8], 71), part),
    }


def shifted(x, lag):
    return jnp.pad(x, ((lag, 0), (0, 0)))[:x.shape[0]]

def advanced(x, lag):
    return jnp.pad(x, ((0, lag), (0, 0)))[lag:]

def short_conv(x, taps):
    return taps[0] * x + taps[1] * shifted(x, 1) + taps[2] * shifted(x, 2)

def short_conv_back(grad, taps):
    return taps[0] * grad + taps[1] * advanced(grad, 1) + taps[2] * advanced(grad, 2)

def spectrum(x):
    return jnp.fft.rfft(x, n=2 * x.shape[0], axis=0)

def restore(spec, length):
    return jnp.fft.irfft(spec, n=2 * length, axis=0)[:length]

def reference(query_proj, key_proj, value_proj, cotangent, boundary, short_taps, skip_gain, long_filter):
    scale = 1.0 / math.sqrt(PAIRS * SEQ_LEN)
    filt_spec = spectrum(long_filter.astype(jnp.float32))
    positions = jnp.arange(SEQ_LEN, dtype=jnp.int32)[:, None]
    filter_sum = jnp.zeros((SEQ_LEN, CH), jnp.float32)
    skip_sum = jnp.zeros((CH,), jnp.float32)
    taps_sum = jnp.zeros((3, 3, CH), jnp.float32)
    outs_q = []
    outs_k = []
    outs_v = []
    for pair in range(PAIRS):
        query = query_proj[pair].astype(jnp.float32)
        keys = key_proj[pair].astype(jnp.float32)
        values = value_proj[pair].astype(jnp.float32)
        conv_q = short_conv(query, short_taps[0])
        conv_k = short_conv(keys, short_taps[1])
        conv_v = short_conv(values, short_taps[2])
        gated = conv_k * conv_v
        gated_spec = spectrum(gated)
        mixed = restore(gated_spec * filt_spec, SEQ_LEN) + skip_gain * gated
        mask = (positions >= boundary[pair]).astype(jnp.float32)
        dout = cotangent[pair].astype(jnp.float32) * mask
        grad_q = dout * mixed
        dmix = dout * conv_q
        dmix_spec = spectrum(dmix)
        dgated = restore(jnp.conj(filt_spec) * dmix_spec, SEQ_LEN) + skip_gain * dmix
        filter_sum = filter_sum + restore(dmix_spec * jnp.conj(gated_spec), SEQ_LEN) * scale
        skip_sum = skip_sum + lax.optimization_barrier(jnp.sum(dmix * gated, axis=0)) * scale
        grad_k = dgated * conv_v
        grad_v = dgated * conv_k
        rows = []
        for branch, (grad, raw) in enumerate(((grad_q, query), (grad_k, keys), (grad_v, values))):
            rows.append(jnp.stack([lax.optimization_barrier(jnp.sum(grad * shifted(raw, lag), axis=0)) for lag in range(3)]))
        taps_sum = taps_sum + jnp.stack(rows) * scale
        outs_q.append(short_conv_back(grad_q, short_taps[0]).astype(jnp.bfloat16))
        outs_k.append(short_conv_back(grad_k, short_taps[1]).astype(jnp.bfloat16))
        outs_v.append(short_conv_back(grad_v, short_taps[2]).astype(jnp.bfloat16))
    return (jnp.stack(outs_q), jnp.stack(outs_k), jnp.stack(outs_v), filter_sum.astype(jnp.bfloat16), taps_sum, skip_sum)
```

```python
import functools
import math

import jax
import jax.numpy as jnp
import numpy as np
from jax import lax
from jax.experimental import pallas as pl
from jax.experimental.pallas import tpu as pltpu
from jax.sharding import PartitionSpec as P

DENSE_LIMIT = 2048


def passed_along(value, axis, by):
    count = lax.axis_size(axis)
    pairs = [(i, i + by) for i in range(count) if 0 <= i + by < count]
    return lax.ppermute(value, axis, pairs)


def matmul_high(form, left, right):
    return jnp.einsum(
        form, left, right, precision=lax.Precision.HIGHEST, preferred_element_type=jnp.float32
    )


def dot_high(left, right):
    return jnp.dot(left, right, precision=lax.Precision.HIGHEST, preferred_element_type=jnp.float32)


def angle_table(left, right, period):
    phase = (left[:, None] * right[None, :] % period).astype(jnp.float32) * (2.0 * math.pi / period)
    return (jnp.cos(phase), jnp.sin(phase))


def build_tables(seq_len):
    cols = min(128, seq_len)
    rows = 2 * seq_len // cols
    half = rows // 2
    keep = half + 1
    col_index = jnp.arange(cols, dtype=jnp.int32)
    keep_index = jnp.arange(keep, dtype=jnp.int32)
    half_index = jnp.arange(half, dtype=jnp.int32)
    col_cos, col_sin = angle_table(col_index, col_index, cols)
    first_cos, first_sin = angle_table(keep_index, half_index, rows)
    first = jnp.stack((first_cos, -first_sin))
    twist_cos, twist_sin = angle_table(keep_index, col_index, 2 * seq_len)
    twist_cos = twist_cos[:, None, :]
    twist_sin = twist_sin[:, None, :]
    fwd_real = jnp.concatenate((col_cos, -col_sin), axis=1)
    fwd_imag = jnp.concatenate((col_sin, col_cos), axis=1)
    inv_real = jnp.concatenate((col_cos, col_sin), axis=1)
    inv_imag = jnp.concatenate((-col_sin, col_cos), axis=1)
    edge = (keep_index == 0) | (keep_index == half)
    weights = jnp.where(edge, 1.0, 2.0).astype(jnp.float32) / (2.0 * seq_len)
    last_cos, last_sin = angle_table(half_index, keep_index, rows)
    last_cos = last_cos * weights[None, :]
    last_sin = last_sin * weights[None, :]
    return (first, twist_cos, twist_sin, fwd_real, fwd_imag, inv_real, inv_imag, last_cos, last_sin)


def forward_half(signal, tables):
    first, twist_cos, twist_sin, fwd_real, fwd_imag = tables[:5]
    width_c, length = signal.shape
    cols = fwd_real.shape[0]
    grid = jnp.transpose(signal.reshape(width_c, length // cols, cols), (1, 0, 2))
    partial_dft = matmul_high("pkn,nca->pkca", first, grid)
    turned_re = partial_dft[0] * twist_cos + partial_dft[1] * twist_sin
    turned_im = partial_dft[1] * twist_cos - partial_dft[0] * twist_sin
    keep = partial_dft.shape[1]
    spec = dot_high(turned_re.reshape(-1, cols), fwd_real) + dot_high(
        turned_im.reshape(-1, cols), fwd_imag
    )
    spec = spec.reshape(keep, width_c, 2, cols)
    return (spec[:, :, 0], spec[:, :, 1])


def inverse_half(spec_re, spec_im, tables):
    twist_cos, twist_sin = (tables[1], tables[2])
    inv_real, inv_imag, last_cos, last_sin = tables[5:]
    keep, width_c, cols = spec_re.shape
    wide = dot_high(spec_re.reshape(-1, cols), inv_real) + dot_high(
        spec_im.reshape(-1, cols), inv_imag
    )
    wide = wide.reshape(keep, width_c, 2, cols)
    wide_re = wide[:, :, 0]
    wide_im = wide[:, :, 1]
    turned_re = wide_re * twist_cos - wide_im * twist_sin
    turned_im = wide_im * twist_cos + wide_re * twist_sin
    grid = matmul_high("nk,kca->nca", last_cos, turned_re) - matmul_high(
        "nk,kca->nca", last_sin, turned_im
    )
    return jnp.transpose(grid, (1, 0, 2)).reshape(width_c, -1)


def convolve_cols(gated_spec, filt_spec, tables):
    gated_re, gated_im = gated_spec
    filt_re, filt_im = filt_spec
    return inverse_half(
        gated_re * filt_re - gated_im * filt_im, gated_re * filt_im + gated_im * filt_re, tables
    )


def correlate_cols(gated_spec, filt_spec, dmix_cols, tables):
    gated_re, gated_im = gated_spec
    filt_re, filt_im = filt_spec
    grad_re, grad_im = forward_half(dmix_cols, tables)
    back = inverse_half(
        filt_re * grad_re + filt_im * grad_im, filt_re * grad_im - filt_im * grad_re, tables
    )
    filt_part = inverse_half(
        grad_re * gated_re + grad_im * gated_im, grad_im * gated_re - grad_re * gated_im, tables
    )
    return (back, filt_part)


def dense_tables(n):
    index = 4 * np.arange(n, dtype=np.int64) + 1
    phase = (index[:, None] * index[None, :] % (16 * n)) * (2.0 * np.pi / (16 * n))
    parts = []
    for table in (np.cos(phase), np.sin(phase)):
        high = table.astype(jnp.bfloat16)
        parts.append(high)
        parts.append((table - high.astype(np.float64)).astype(jnp.bfloat16))
    turn = index * (2.0 * np.pi / (16 * n))
    twist = np.stack((np.cos(turn), np.sin(turn)))[:, :, None].astype(np.float32)
    return tuple(parts), twist


def split_to(ref, lead, rows, value):
    high = value.astype(jnp.bfloat16)
    ref[(*lead, 0, rows)] = high
    ref[(*lead, 1, rows)] = (value - high.astype(jnp.float32)).astype(jnp.bfloat16)


def dot(left, right):
    return jnp.dot(left, right, preferred_element_type=jnp.float32)


def dot3(high, low, ref, lead):
    top = ref[(*lead, 0)]
    return dot(high, top) + (dot(high, ref[(*lead, 1)]) + dot(low, top))


def operator_steps(
    n, scale, bound, q, k, v, c, h, taps, skip, tables, twist, outs, filt, tsum, ssum, scratch
):
    chi, clo, shi, slo = tables
    gd, spec, s1s, s2s, dms, ds = scratch
    width = q.shape[1]
    rows = 64
    rt = lambda b, j: taps[pl.ds(3 * b + j, 1), :]

    def lagged(ref, i):
        base = pl.multiple_of(i * rows, rows)
        head = pl.multiple_of(jnp.maximum(base - 16, 0), 16)
        halo = ref[pl.ds(head, 16), :].astype(jnp.float32)
        halo = jnp.where(i > 0, halo, 0.0)
        ext = jnp.concatenate((halo, ref[pl.ds(base, rows), :].astype(jnp.float32)), axis=0)
        return ext[16:], pltpu.roll(ext, 1, 0)[16:], pltpu.roll(ext, 2, 0)[16:]

    def short(ref, b, i):
        x0, x1, x2 = lagged(ref, i)
        return rt(b, 0) * x0 + rt(b, 1) * x1 + rt(b, 2) * x2

    def masked(i):
        base = pl.multiple_of(i * rows, rows)
        pos = base + lax.broadcasted_iota(jnp.int32, (rows, width), 0)
        return jnp.where(pos >= bound, c[pl.ds(base, rows), :].astype(jnp.float32), 0.0)

    ssum[...] = jnp.zeros_like(ssum)
    tsum[...] = jnp.zeros_like(tsum)

    @pl.loop(0, n // rows)
    def _(i):
        at = pl.ds(pl.multiple_of(i * rows, rows), rows)
        s1 = short(k, 1, i)
        s2 = short(v, 2, i)
        gated = s1 * s2
        dmix = masked(i) * short(q, 0, i)
        s1s[at, :] = s1
        s2s[at, :] = s2
        dms[at, :] = dmix
        split_to(gd, (0,), at, gated)
        split_to(gd, (1,), at, dmix)
        ssum[...] += jnp.sum((dmix * gated).reshape(rows // 8, 8, width), axis=0)

    block = min(256, n)

    @pl.loop(0, n // block)
    def _(j):
        at = pl.ds(pl.multiple_of(j * block, block), block)
        ch, cl, sh, sl = chi[at, :], clo[at, :], shi[at, :], slo[at, :]
        tr, ti = twist[0, at, :], twist[1, at, :]
        hr = dot(ch, h[...]) + dot(cl, h[...])
        hi = -(dot(sh, h[...]) + dot(sl, h[...]))
        hr, hi = hr * tr - hi * ti, hr * ti + hi * tr
        gr = dot3(ch, cl, gd, (0,))
        gi = -dot3(sh, sl, gd, (0,))
        split_to(spec, (0, 0), at, gr * hr - gi * hi)
        split_to(spec, (0, 1), at, gr * hi + gi * hr)
        gr, gi = gr * tr - gi * ti, gr * ti + gi * tr
        dr = dot3(ch, cl, gd, (1,))
        di = -dot3(sh, sl, gd, (1,))
        split_to(spec, (1, 0), at, hr * dr + hi * di)
        split_to(spec, (1, 1), at, hr * di - hi * dr)
        split_to(spec, (2, 0), at, gr * dr + gi * di)
        split_to(spec, (2, 1), at, gr * di - gi * dr)

    @pl.loop(0, n // block)
    def _(j):
        at = pl.ds(pl.multiple_of(j * block, block), block)
        ch, cl, sh, sl = chi[at, :], clo[at, :], shi[at, :], slo[at, :]
        filt[at, :] = (
            dot3(ch, cl, spec, (2, 0)) - dot3(sh, sl, spec, (2, 1))
        ) * (scale / n)
        ds[0, at, :] = (dot3(ch, cl, spec, (0, 0)) - dot3(sh, sl, spec, (0, 1))) * (1.0 / n)
        ds[1, at, :] = (dot3(ch, cl, spec, (1, 0)) - dot3(sh, sl, spec, (1, 1))) * (1.0 / n)

    ds[:, pl.ds(n, 8), :] = jnp.zeros((3, 8, width), jnp.float32)

    @pl.loop(0, n // rows)
    def _(i):
        at = pl.ds(pl.multiple_of(i * rows, rows), rows)
        s1, s2, dmix = s1s[at, :], s2s[at, :], dms[at, :]
        d0 = masked(i) * (ds[0, at, :] + skip[...] * (s1 * s2))
        dg = ds[1, at, :] + skip[...] * dmix
        for b, (d, ref) in enumerate(((d0, q), (dg * s2, k), (dg * s1, v))):
            ds[b, at, :] = d
            for lag, x in enumerate(lagged(ref, i)):
                tsum[3 * b + lag] += jnp.sum((d * x).reshape(rows // 8, 8, width), axis=0)

    @pl.loop(0, n // rows)
    def _(i):
        base = pl.multiple_of(i * rows, rows)
        for b in range(3):
            ext = ds[b, pl.ds(base, rows + 8), :]
            g = rt(b, 0) * ext + rt(b, 1) * pltpu.roll(ext, rows + 7, 0)
            g = g + rt(b, 2) * pltpu.roll(ext, rows + 6, 0)
            outs[b][pl.ds(base, rows), :] = g[:rows].astype(jnp.bfloat16)


def operator_kernel(n, scale, bound, q, k, v, c, h, taps, skip, *rest):
    tables, twist = rest[:4], rest[4]
    outs, filt, tsum, ssum = rest[5:8], rest[8], rest[9], rest[10]
    operator_steps(
        n, scale, bound[0], q, k, v, c, h, taps, skip, tables, twist, outs, filt, tsum, ssum, rest[11:]
    )


def scratch_of(n, width):
    return [
        pltpu.VMEM((2, 2, n, width), jnp.bfloat16),
        pltpu.VMEM((3, 2, 2, n, width), jnp.bfloat16),
        pltpu.VMEM((n, width), jnp.float32),
        pltpu.VMEM((n, width), jnp.float32),
        pltpu.VMEM((n, width), jnp.float32),
        pltpu.VMEM((3, n + 8, width), jnp.float32),
    ]


def to_owner(value):
    return lax.all_to_all(value, "seq", split_axis=1, concat_axis=0, tiled=True)


def to_rows(value):
    return lax.all_to_all(value, "seq", split_axis=0, concat_axis=1, tiled=True)


def dense_body(query_proj, key_proj, value_proj, cotangent, boundary, short_taps, skip_gain, long_filter):
    tok, width = query_proj.shape[1:]
    parts = lax.axis_size("seq")
    n = tok * parts
    own = width // parts
    scale = 1.0 / math.sqrt(lax.axis_size("dp") * n)
    tables, twist = dense_tables(n)
    first = lax.axis_index("seq") * own
    taps = lax.dynamic_slice_in_dim(short_taps.reshape(9, width), first, own, axis=1)
    skip = lax.dynamic_slice_in_dim(skip_gain[None], first, own, axis=1)
    cols = [to_owner(x[0]) for x in (query_proj, key_proj, value_proj, cotangent)]
    vmem = pl.BlockSpec(memory_space=pltpu.VMEM)
    f32, bf16 = jnp.float32, jnp.bfloat16
    gq, gk, gv, filt, tsum, ssum = pl.pallas_call(
        functools.partial(operator_kernel, n, scale),
        out_shape=[jax.ShapeDtypeStruct((n, own), bf16)] * 3
        + [
            jax.ShapeDtypeStruct((n, own), f32),
            jax.ShapeDtypeStruct((9, 8, own), f32),
            jax.ShapeDtypeStruct((8, own), f32),
        ],
        in_specs=[pl.BlockSpec(memory_space=pltpu.SMEM)] + [vmem] * 12,
        out_specs=[vmem] * 6,
        scratch_shapes=scratch_of(n, own),
        compiler_params=pltpu.CompilerParams(vmem_limit_bytes=56 * 2**20),
    )(boundary, *cols, to_owner(long_filter), taps, skip, *(jnp.asarray(t) for t in tables), jnp.asarray(twist))
    sums = jnp.concatenate((jnp.sum(tsum, axis=1), jnp.sum(ssum, axis=0, keepdims=True))) * scale
    pair = [(0, 1), (1, 0)]
    filt = filt + lax.ppermute(filt, "dp", pair)
    sums = sums + lax.ppermute(sums, "dp", pair)
    filter_grad = to_rows(filt.astype(bf16))
    grads = [to_rows(g)[None] for g in (gq, gk, gv)]
    return (*grads, filter_grad, sums[:9].reshape(3, 3, own), sums[9])


def body(query_proj, key_proj, value_proj, cotangent, boundary, short_taps, skip_gain, long_filter):
    pairs, tok, width = query_proj.shape
    parts = lax.axis_size("seq")
    seq_len = tok * parts
    scale = 1.0 / math.sqrt(pairs * lax.axis_size("dp") * seq_len)
    tables = build_tables(seq_len)
    filter_cols = lax.all_to_all(
        jnp.transpose(long_filter), "seq", split_axis=0, concat_axis=1, tiled=True
    ).astype(jnp.float32)
    filt_spec = forward_half(filter_cols, tables)
    taps = short_taps[:, :, None, None, :]
    raw = jnp.stack((query_proj, key_proj, value_proj))
    tails = passed_along(raw[:, :, tok - 2 :], "seq", 1)
    extended = jnp.concatenate((tails, raw), axis=2).astype(jnp.float32)
    conv = (
        taps[:, 0] * extended[:, :, 2:]
        + taps[:, 1] * extended[:, :, 1:-1]
        + taps[:, 2] * extended[:, :, :-2]
    )
    gated = conv[1] * conv[2]
    position = lax.axis_index("seq") * tok + jnp.arange(tok, dtype=jnp.int32)
    mask = (position[None, :] >= boundary[:, None]).astype(jnp.float32)
    dout = cotangent.astype(jnp.float32) * mask[:, :, None]
    dmix = dout * conv[0]
    gated_cols = lax.all_to_all(
        jnp.transpose(gated, (0, 2, 1)), "seq", split_axis=1, concat_axis=2, tiled=True
    )
    spectra = forward_half(gated_cols[0], tables)
    conv_cols = jnp.stack([convolve_cols(spectra, filt_spec, tables)])
    conv_rows = lax.all_to_all(conv_cols, "seq", split_axis=2, concat_axis=1, tiled=True)
    dmix_cols = lax.all_to_all(
        jnp.transpose(dmix, (0, 2, 1)), "seq", split_axis=1, concat_axis=2, tiled=True
    )
    back_cols, filt_part = correlate_cols(spectra, filt_spec, dmix_cols[0], tables)
    back_list = [back_cols]
    filt_list = [filt_part]
    back_rows = lax.all_to_all(jnp.stack(back_list), "seq", split_axis=2, concat_axis=1, tiled=True)
    mixed = jnp.transpose(conv_rows, (0, 2, 1)) + skip_gain * gated
    filter_part = jnp.sum(jnp.stack(filt_list), axis=0) * scale
    filter_total = lax.psum(filter_part, "dp")
    filter_rows = lax.all_to_all(
        filter_total.astype(jnp.bfloat16), "seq", split_axis=1, concat_axis=0, tiled=True
    )
    filter_grad = jnp.transpose(filter_rows)
    dgated = jnp.transpose(back_rows, (0, 2, 1)) + skip_gain * dmix
    upstream = jnp.stack((dout * mixed, dgated * conv[2], dgated * conv[1]))
    heads = passed_along(upstream[:, :, :2], "seq", -1)
    grad_ext = jnp.concatenate((upstream, heads), axis=2)
    grads = (
        taps[:, 0] * grad_ext[:, :, :tok]
        + taps[:, 1] * grad_ext[:, :, 1 : tok + 1]
        + taps[:, 2] * grad_ext[:, :, 2:]
    )
    grads = grads.astype(jnp.bfloat16)
    taps_part = (
        jnp.stack(
            [
                jnp.sum(upstream * extended[:, :, 2 - lag : 2 - lag + tok], axis=(1, 2))
                for lag in range(3)
            ],
            axis=1,
        )
        * scale
    )
    skip_part = jnp.sum(dmix * gated, axis=(0, 1)) * scale
    taps_local, skip_local = (
        lax.psum_scatter(taps_part, "seq", scatter_dimension=2, tiled=True),
        lax.psum_scatter(skip_part, "seq", scatter_dimension=0, tiled=True),
    )
    taps_grad, skip_grad = lax.psum((taps_local, skip_local), "dp")
    return (grads[0], grads[1], grads[2], filter_grad, taps_grad, skip_grad)


def solution(mesh):
    in_specs = (
        P(("groups", "dp"), "seq", None),
        P(("groups", "dp"), "seq", None),
        P(("groups", "dp"), "seq", None),
        P(("groups", "dp"), "seq", None),
        P(("groups", "dp")),
        P(),
        P(),
        P("seq", None),
    )
    out_specs = (
        P(("groups", "dp"), "seq", None),
        P(("groups", "dp"), "seq", None),
        P(("groups", "dp"), "seq", None),
        P(("groups", "seq"), None),
        P("groups", None, "seq"),
        P(("groups", "seq")),
    )
    def chosen(query_proj, *rest):
        pairs, tok, _ = query_proj.shape
        dense = pairs == 1 and mesh.shape["dp"] == 2 and tok * mesh.shape["seq"] <= DENSE_LIMIT
        return (dense_body if dense else body)(query_proj, *rest)

    return jax.shard_map(chosen, mesh=mesh, in_specs=in_specs, out_specs=out_specs, check_vma=False)
```

```python
import functools
import math

import jax
import jax.numpy as jnp
import numpy as np
from jax import lax
from jax.experimental import pallas as pl
from jax.experimental.pallas import tpu as pltpu
from jax.sharding import PartitionSpec as P

DENSE_LIMIT = 1024
LANES = 128
MESH = pl.DeviceIdType.MESH


def passed_along(value, axis, by):
    count = lax.axis_size(axis)
    pairs = [(i, i + by) for i in range(count) if 0 <= i + by < count]
    return lax.ppermute(value, axis, pairs)


def matmul_high(form, left, right):
    return jnp.einsum(
        form, left, right, precision=lax.Precision.HIGHEST, preferred_element_type=jnp.float32
    )


def dot_high(left, right):
    return jnp.dot(left, right, precision=lax.Precision.HIGHEST, preferred_element_type=jnp.float32)


def angle_table(left, right, period):
    phase = (left[:, None] * right[None, :] % period).astype(jnp.float32) * (2.0 * math.pi / period)
    return (jnp.cos(phase), jnp.sin(phase))


def build_tables(seq_len):
    cols = min(128, seq_len)
    rows = 2 * seq_len // cols
    half = rows // 2
    keep = half + 1
    col_index = jnp.arange(cols, dtype=jnp.int32)
    keep_index = jnp.arange(keep, dtype=jnp.int32)
    half_index = jnp.arange(half, dtype=jnp.int32)
    col_cos, col_sin = angle_table(col_index, col_index, cols)
    first_cos, first_sin = angle_table(keep_index, half_index, rows)
    first = jnp.stack((first_cos, -first_sin))
    twist_cos, twist_sin = angle_table(keep_index, col_index, 2 * seq_len)
    twist_cos = twist_cos[:, None, :]
    twist_sin = twist_sin[:, None, :]
    fwd_real = jnp.concatenate((col_cos, -col_sin), axis=1)
    fwd_imag = jnp.concatenate((col_sin, col_cos), axis=1)
    inv_real = jnp.concatenate((col_cos, col_sin), axis=1)
    inv_imag = jnp.concatenate((-col_sin, col_cos), axis=1)
    edge = (keep_index == 0) | (keep_index == half)
    weights = jnp.where(edge, 1.0, 2.0).astype(jnp.float32) / (2.0 * seq_len)
    last_cos, last_sin = angle_table(half_index, keep_index, rows)
    last_cos = last_cos * weights[None, :]
    last_sin = last_sin * weights[None, :]
    return (first, twist_cos, twist_sin, fwd_real, fwd_imag, inv_real, inv_imag, last_cos, last_sin)


def forward_half(signal, tables):
    first, twist_cos, twist_sin, fwd_real, fwd_imag = tables[:5]
    width_c, length = signal.shape
    cols = fwd_real.shape[0]
    grid = jnp.transpose(signal.reshape(width_c, length // cols, cols), (1, 0, 2))
    partial_dft = matmul_high("pkn,nca->pkca", first, grid)
    turned_re = partial_dft[0] * twist_cos + partial_dft[1] * twist_sin
    turned_im = partial_dft[1] * twist_cos - partial_dft[0] * twist_sin
    keep = partial_dft.shape[1]
    spec = dot_high(turned_re.reshape(-1, cols), fwd_real) + dot_high(
        turned_im.reshape(-1, cols), fwd_imag
    )
    spec = spec.reshape(keep, width_c, 2, cols)
    return (spec[:, :, 0], spec[:, :, 1])


def inverse_half(spec_re, spec_im, tables):
    twist_cos, twist_sin = (tables[1], tables[2])
    inv_real, inv_imag, last_cos, last_sin = tables[5:]
    keep, width_c, cols = spec_re.shape
    wide = dot_high(spec_re.reshape(-1, cols), inv_real) + dot_high(
        spec_im.reshape(-1, cols), inv_imag
    )
    wide = wide.reshape(keep, width_c, 2, cols)
    wide_re = wide[:, :, 0]
    wide_im = wide[:, :, 1]
    turned_re = wide_re * twist_cos - wide_im * twist_sin
    turned_im = wide_im * twist_cos + wide_re * twist_sin
    grid = matmul_high("nk,kca->nca", last_cos, turned_re) - matmul_high(
        "nk,kca->nca", last_sin, turned_im
    )
    return jnp.transpose(grid, (1, 0, 2)).reshape(width_c, -1)


def convolve_cols(gated_spec, filt_spec, tables):
    gated_re, gated_im = gated_spec
    filt_re, filt_im = filt_spec
    return inverse_half(
        gated_re * filt_re - gated_im * filt_im, gated_re * filt_im + gated_im * filt_re, tables
    )


def correlate_cols(gated_spec, filt_spec, dmix_cols, tables):
    gated_re, gated_im = gated_spec
    filt_re, filt_im = filt_spec
    grad_re, grad_im = forward_half(dmix_cols, tables)
    back = inverse_half(
        filt_re * grad_re + filt_im * grad_im, filt_re * grad_im - filt_im * grad_re, tables
    )
    filt_part = inverse_half(
        grad_re * gated_re + grad_im * gated_im, grad_im * gated_re - grad_re * gated_im, tables
    )
    return (back, filt_part)


def phase_tables(n):
    index = 4 * np.arange(n, dtype=np.int64) + 1
    unit = 2.0 * np.pi / (16 * n)
    fine = (index[:, None] * index[None, :LANES] % (16 * n)) * unit
    coarse = (index[:, None] * (4 * LANES * np.arange(n // LANES))[None, :] % (16 * n)) * unit
    turn = index[:, None] * unit
    pack = lambda x: np.stack((np.cos(x), np.sin(x))).astype(np.float32)
    return pack(fine), pack(np.concatenate((coarse, turn), axis=1))


def split_to(ref, lead, rows, value, cols=slice(None)):
    high = value.astype(jnp.bfloat16)
    ref[(*lead, 0, rows, cols)] = high
    ref[(*lead, 1, rows, cols)] = (value - high.astype(jnp.float32)).astype(jnp.bfloat16)


def dot(left, right):
    return jnp.dot(left, right, preferred_element_type=jnp.float32)


def dot3(high, low, ref, lead):
    top = ref[(*lead, 0)]
    return dot(high, top) + (dot(high, ref[(*lead, 1)]) + dot(low, top))


def operator_kernel(
    n, parts, scale, bound, q_in, k_in, v_in, c_in, h_in, taps_in, skip_in, fine, coarse,
    gq_out, gk_out, gv_out, f_out, taps_out, skip_out,
    bufs, cosines, sines, gd, spec, hspec, gspec, s1s, s2s, dms, ds, filt, fother, fown, stage,
    taps, sums, sother, tsum, send_sem, recv_sem, local_sem, dp_send, dp_recv,
):
    tok = n // parts
    width = bufs.shape[2]
    half = width // 2
    rows = 64
    block = min(256, n)
    me = lax.axis_index("seq")
    core = lax.axis_index("dp")
    partner = {"dp": 1 - core}
    f32, bf16 = jnp.float32, jnp.bfloat16
    mine = pl.ds(pl.multiple_of(me * tok, tok), tok)
    my_half = pl.ds(pl.multiple_of(core * half, half), half)
    other_half = pl.ds(pl.multiple_of((1 - core) * half, half), half)

    def cols_of(owner):
        return pl.ds(pl.multiple_of(owner * width, width), width)

    def half_cols_of(owner):
        return pl.ds(pl.multiple_of(owner * width + core * half, half), half)

    peers = [lax.rem(me + s, parts) for s in range(parts)]

    barrier = pltpu.get_barrier_semaphore()
    for s in range(1, parts):
        pl.semaphore_signal(barrier, inc=1, device_id={"seq": peers[s]}, device_id_type=MESH)
    pl.semaphore_signal(barrier, inc=1, device_id=partner, device_id_type=MESH)
    pl.semaphore_wait(barrier, parts)

    def exchange(a, source, target):
        own = pltpu.make_async_copy(source(me), target, local_sem.at[a])
        own.start()
        copies = []
        for s in range(1, parts):
            copy = pltpu.make_async_remote_copy(
                src_ref=source(peers[s]),
                dst_ref=target,
                send_sem=send_sem.at[a, s],
                recv_sem=recv_sem.at[a, s],
                device_id={"seq": peers[s]},
                device_id_type=MESH,
            )
            copy.start()
            copies.append(copy)
        return own, copies

    def arrived(moved):
        moved[0].wait()
        for copy in moved[1]:
            copy.wait_recv()

    def to_partner(i, source, target):
        return pltpu.make_async_remote_copy(
            src_ref=source,
            dst_ref=target,
            send_sem=dp_send.at[i],
            recv_sem=dp_recv.at[i],
            device_id=partner,
            device_id_type=MESH,
        )

    hb, kb, vb, qb, cb = (bufs.at[i] for i in range(5))
    h_moved = exchange(0, lambda o: h_in.at[:, half_cols_of(o)], hb.at[mine, my_half])
    ins = [
        exchange(1 + i, lambda o, x=x: x.at[0, :, cols_of(o)], bufs.at[1 + i, mine, :])
        for i, x in enumerate((k_in, v_in, q_in, c_in))
    ]

    own_cols = cols_of(me)
    taps[pl.ds(0, 9), :] = taps_in[:, own_cols]
    taps[pl.ds(9, 1), :] = skip_in[:, own_cols]
    tsum[...] = jnp.zeros_like(tsum)
    ds[:, pl.ds(n, 8), :] = jnp.zeros((3, 8, width), f32)

    @pl.loop(0, n // rows)
    def _(i):
        at = pl.ds(pl.multiple_of(i * rows, rows), rows)
        fr, fi = fine[0, at, :], fine[1, at, :]
        cr, ci = coarse[0, at, :], coarse[1, at, :]
        for a in range(n // LANES):
            ar, ai = cr[:, a : a + 1], ci[:, a : a + 1]
            cols = slice(a * LANES, (a + 1) * LANES)
            split_to(cosines, (), at, fr * ar - fi * ai, cols)
            split_to(sines, (), at, fr * ai + fi * ar, cols)

    def tap(b, j):
        return taps[pl.ds(3 * b + j, 1), :]

    def gain():
        return taps[pl.ds(9, 1), :]

    def at_rows(i):
        return pl.ds(pl.multiple_of(i * rows, rows), rows)

    def lagged(ref, i):
        head = pl.multiple_of(jnp.maximum(i * rows - 16, 0), 16)
        halo = jnp.where(i > 0, ref[pl.ds(head, 16), :].astype(f32), 0.0)
        ext = jnp.concatenate((halo, ref[at_rows(i), :].astype(f32)), axis=0)
        return ext[16:], pltpu.roll(ext, 1, 0)[16:], pltpu.roll(ext, 2, 0)[16:]

    def short(b, lags):
        return tap(b, 0) * lags[0] + tap(b, 1) * lags[1] + tap(b, 2) * lags[2]

    def add_sum(i, value):
        tsum[i] += jnp.sum(value.reshape(rows // 8, 8, width), axis=0)

    def add_taps(b, d, lags):
        for j in range(3):
            add_sum(3 * b + j, d * lags[j])

    def short_back(b):
        @pl.loop(0, n // rows)
        def _(i):
            ext = ds[b, pl.ds(pl.multiple_of(i * rows, rows), rows + 8), :]
            g = tap(b, 0) * ext + tap(b, 1) * pltpu.roll(ext, rows + 7, 0)
            g = g + tap(b, 2) * pltpu.roll(ext, rows + 6, 0)
            stage[b, at_rows(i), :] = g[:rows].astype(bf16)

    def blocks(table, at):
        return table[0, at, :], table[1, at, :]

    def inverse(b, at):
        ch, cl = blocks(cosines, at)
        sh, sl = blocks(sines, at)
        return dot3(ch, cl, spec, (b, 0)) - dot3(sh, sl, spec, (b, 1))

    def turned(at, re, im):
        last = coarse.shape[2] - 1
        tr, ti = coarse[0, at, last:], coarse[1, at, last:]
        return re * tr - im * ti, re * ti + im * tr

    def at_block(j):
        return pl.ds(pl.multiple_of(j * block, block), block)

    arrived(h_moved)
    h_relay = to_partner(0, hb.at[:, my_half], hb.at[:, my_half])
    h_relay.start()
    arrived(ins[0])
    arrived(ins[1])

    @pl.loop(0, n // rows)
    def _(i):
        at = at_rows(i)
        s1 = short(1, lagged(kb, i))
        s2 = short(2, lagged(vb, i))
        s1s[at, :] = s1
        s2s[at, :] = s2
        split_to(gd, (0,), at, s1 * s2)

    h_relay.wait_recv()

    @pl.loop(0, n // block)
    def _(j):
        at = at_block(j)
        ch, cl = blocks(cosines, at)
        sh, sl = blocks(sines, at)
        h = hb[...]
        hr, hi = turned(at, dot(ch, h) + dot(cl, h), -(dot(sh, h) + dot(sl, h)))
        hspec[0, at, :], hspec[1, at, :] = hr, hi
        gr, gi = dot3(ch, cl, gd, (0,)), -dot3(sh, sl, gd, (0,))
        split_to(spec, (0, 0), at, gr * hr - gi * hi)
        split_to(spec, (0, 1), at, gr * hi + gi * hr)
        gspec[0, at, :], gspec[1, at, :] = turned(at, gr, gi)

    @pl.loop(0, n // block)
    def _(j):
        at = at_block(j)
        ds[0, at, :] = inverse(0, at) * (1.0 / n)

    arrived(ins[2])
    arrived(ins[3])

    @pl.loop(0, n // rows)
    def _(i):
        at = at_rows(i)
        pos = i * rows + lax.broadcasted_iota(jnp.int32, (rows, width), 0)
        dout = jnp.where(pos >= bound[0], cb[at, :].astype(f32), 0.0)
        gated = s1s[at, :] * s2s[at, :]
        lags = lagged(qb, i)
        dmix = dout * short(0, lags)
        d = dout * (ds[0, at, :] + gain() * gated)
        ds[0, at, :] = d
        dms[at, :] = dmix
        split_to(gd, (1,), at, dmix)
        add_sum(9, dmix * gated)
        add_taps(0, d, lags)

    def send_back(b, out):
        short_back(b)
        return exchange(5 + b, lambda o: stage.at[b, rows_of(o), :], out.at[0, :, own_cols])

    def rows_of(owner):
        return pl.ds(pl.multiple_of(owner * tok, tok), tok)

    gq_moved = send_back(0, gq_out)

    @pl.loop(0, n // block)
    def _(j):
        at = at_block(j)
        ch, cl = blocks(cosines, at)
        sh, sl = blocks(sines, at)
        dr, di = dot3(ch, cl, gd, (1,)), -dot3(sh, sl, gd, (1,))
        hr, hi = hspec[0, at, :], hspec[1, at, :]
        split_to(spec, (1, 0), at, hr * dr + hi * di)
        split_to(spec, (1, 1), at, hr * di - hi * dr)
        gr, gi = gspec[0, at, :], gspec[1, at, :]
        split_to(spec, (2, 0), at, gr * dr + gi * di)
        split_to(spec, (2, 1), at, gr * di - gi * dr)

    @pl.loop(0, n // block)
    def _(j):
        at = at_block(j)
        ds[1, at, :] = inverse(1, at) * (1.0 / n)

    @pl.loop(0, n // rows)
    def _(i):
        at = at_rows(i)
        dg = ds[1, at, :] + gain() * dms[at, :]
        for b, other, ref in ((1, s2s, kb), (2, s1s, vb)):
            d = dg * other[at, :]
            ds[b, at, :] = d
            add_taps(b, d, lagged(ref, i))

    gk_moved = send_back(1, gk_out)
    gv_moved = send_back(2, gv_out)

    @pl.loop(0, n // block)
    def _(j):
        at = at_block(j)
        filt[at, :] = inverse(2, at) * (scale / n)

    f_add = to_partner(1, filt.at[:, other_half], fother)
    f_add.start()
    sums[...] = jnp.zeros_like(sums)
    sums[pl.ds(0, 10), :] = jnp.sum(tsum[...], axis=1) * scale
    s_add = to_partner(2, sums, sother)
    s_add.start()
    f_add.wait_recv()

    @pl.loop(0, n // rows)
    def _(i):
        at = at_rows(i)
        fown[at, :] = (filt[at, my_half] + fother[at, :]).astype(bf16)

    f_moved = exchange(8, lambda o: fown.at[rows_of(o), :], f_out.at[:, half_cols_of(me)])
    own_relay = to_partner(3, fown.at[mine, :], f_out.at[:, half_cols_of(me)])
    own_relay.start()
    s_add.wait_recv()
    total = sums[...] + sother[...]
    for b in range(3):
        taps_out[b] = total[3 * b : 3 * b + 3]
    skip_out[...] = total[9:10]

    relays = [own_relay]
    for s in range(1, parts):
        f_moved[1][s - 1].wait_recv()
        block_cols = half_cols_of(lax.rem(me + parts - s, parts))
        relay = to_partner(3 + s, f_out.at[:, block_cols], f_out.at[:, block_cols])
        relay.start()
        relays.append(relay)
    f_moved[0].wait()
    for moved in (gq_moved, gk_moved, gv_moved):
        arrived(moved)
    for relay in relays:
        relay.wait_recv()
    for moved in (h_moved, *ins, gq_moved, gk_moved, gv_moved, f_moved):
        for copy in moved[1]:
            copy.wait_send()
    for copy in (h_relay, f_add, s_add, *relays):
        copy.wait_send()


def dense_body(query_proj, key_proj, value_proj, cotangent, boundary, short_taps, skip_gain, long_filter):
    tok, width = query_proj.shape[1:]
    parts = lax.axis_size("seq")
    n = tok * parts
    own = width // parts
    scale = 1.0 / math.sqrt(lax.axis_size("dp") * n)
    fine, coarse = phase_tables(n)
    vmem = pl.BlockSpec(memory_space=pltpu.VMEM)
    anywhere = pl.BlockSpec(memory_space=pl.ANY)
    f32, bf16 = jnp.float32, jnp.bfloat16
    shape = jax.ShapeDtypeStruct
    dma = pltpu.SemaphoreType.DMA
    gq, gk, gv, filter_grad, taps_grad, skip_grad = pl.pallas_call(
        functools.partial(operator_kernel, n, parts, scale),
        out_shape=[shape((1, tok, width), bf16)] * 3
        + [shape((tok, width), bf16), shape((3, 3, own), f32), shape((1, own), f32)],
        in_specs=[pl.BlockSpec(memory_space=pltpu.SMEM)] + [anywhere] * 5 + [vmem] * 4,
        out_specs=[anywhere] * 4 + [vmem] * 2,
        scratch_shapes=[
            pltpu.VMEM((5, n, own), bf16),
            pltpu.VMEM((2, n, n), bf16),
            pltpu.VMEM((2, n, n), bf16),
            pltpu.VMEM((2, 2, n, own), bf16),
            pltpu.VMEM((3, 2, 2, n, own), bf16),
            pltpu.VMEM((2, n, own), f32),
            pltpu.VMEM((2, n, own), f32),
            pltpu.VMEM((n, own), f32),
            pltpu.VMEM((n, own), f32),
            pltpu.VMEM((n, own), f32),
            pltpu.VMEM((3, n + 8, own), f32),
            pltpu.VMEM((n, own), f32),
            pltpu.VMEM((n, own // 2), f32),
            pltpu.VMEM((n, own // 2), bf16),
            pltpu.VMEM((3, n, own), bf16),
            pltpu.VMEM((16, own), f32),
            pltpu.VMEM((16, own), f32),
            pltpu.VMEM((16, own), f32),
            pltpu.VMEM((10, 8, own), f32),
            dma((9, parts)),
            dma((9, parts)),
            dma((9,)),
            dma((3 + parts,)),
            dma((3 + parts,)),
        ],
        compiler_params=pltpu.CompilerParams(
            collective_id=0, has_side_effects=True, vmem_limit_bytes=56 * 2**20
        ),
    )(
        boundary, query_proj, key_proj, value_proj, cotangent, long_filter,
        short_taps.reshape(9, width), skip_gain[None], jnp.asarray(fine), jnp.asarray(coarse),
    )
    return gq, gk, gv, filter_grad, taps_grad, skip_grad.reshape(own)


def body(query_proj, key_proj, value_proj, cotangent, boundary, short_taps, skip_gain, long_filter):
    pairs, tok, width = query_proj.shape
    parts = lax.axis_size("seq")
    seq_len = tok * parts
    scale = 1.0 / math.sqrt(pairs * lax.axis_size("dp") * seq_len)
    tables = build_tables(seq_len)
    filter_cols = lax.all_to_all(
        jnp.transpose(long_filter), "seq", split_axis=0, concat_axis=1, tiled=True
    ).astype(jnp.float32)
    filt_spec = forward_half(filter_cols, tables)
    taps = short_taps[:, :, None, None, :]
    raw = jnp.stack((query_proj, key_proj, value_proj))
    tails = passed_along(raw[:, :, tok - 2 :], "seq", 1)
    extended = jnp.concatenate((tails, raw), axis=2).astype(jnp.float32)
    conv = (
        taps[:, 0] * extended[:, :, 2:]
        + taps[:, 1] * extended[:, :, 1:-1]
        + taps[:, 2] * extended[:, :, :-2]
    )
    gated = conv[1] * conv[2]
    position = lax.axis_index("seq") * tok + jnp.arange(tok, dtype=jnp.int32)
    mask = (position[None, :] >= boundary[:, None]).astype(jnp.float32)
    dout = cotangent.astype(jnp.float32) * mask[:, :, None]
    dmix = dout * conv[0]
    gated_cols = lax.all_to_all(
        jnp.transpose(gated, (0, 2, 1)), "seq", split_axis=1, concat_axis=2, tiled=True
    )
    spectra = forward_half(gated_cols[0], tables)
    conv_cols = jnp.stack([convolve_cols(spectra, filt_spec, tables)])
    conv_rows = lax.all_to_all(conv_cols, "seq", split_axis=2, concat_axis=1, tiled=True)
    dmix_cols = lax.all_to_all(
        jnp.transpose(dmix, (0, 2, 1)), "seq", split_axis=1, concat_axis=2, tiled=True
    )
    back_cols, filt_part = correlate_cols(spectra, filt_spec, dmix_cols[0], tables)
    back_list = [back_cols]
    filt_list = [filt_part]
    back_rows = lax.all_to_all(jnp.stack(back_list), "seq", split_axis=2, concat_axis=1, tiled=True)
    mixed = jnp.transpose(conv_rows, (0, 2, 1)) + skip_gain * gated
    filter_part = jnp.sum(jnp.stack(filt_list), axis=0) * scale
    filter_total = lax.psum(filter_part, "dp")
    filter_rows = lax.all_to_all(
        filter_total.astype(jnp.bfloat16), "seq", split_axis=1, concat_axis=0, tiled=True
    )
    filter_grad = jnp.transpose(filter_rows)
    dgated = jnp.transpose(back_rows, (0, 2, 1)) + skip_gain * dmix
    upstream = jnp.stack((dout * mixed, dgated * conv[2], dgated * conv[1]))
    heads = passed_along(upstream[:, :, :2], "seq", -1)
    grad_ext = jnp.concatenate((upstream, heads), axis=2)
    grads = (
        taps[:, 0] * grad_ext[:, :, :tok]
        + taps[:, 1] * grad_ext[:, :, 1 : tok + 1]
        + taps[:, 2] * grad_ext[:, :, 2:]
    )
    grads = grads.astype(jnp.bfloat16)
    taps_part = (
        jnp.stack(
            [
                jnp.sum(upstream * extended[:, :, 2 - lag : 2 - lag + tok], axis=(1, 2))
                for lag in range(3)
            ],
            axis=1,
        )
        * scale
    )
    skip_part = jnp.sum(dmix * gated, axis=(0, 1)) * scale
    taps_local, skip_local = (
        lax.psum_scatter(taps_part, "seq", scatter_dimension=2, tiled=True),
        lax.psum_scatter(skip_part, "seq", scatter_dimension=0, tiled=True),
    )
    taps_grad, skip_grad = lax.psum((taps_local, skip_local), "dp")
    return (grads[0], grads[1], grads[2], filter_grad, taps_grad, skip_grad)


def solution(mesh):
    in_specs = (
        P(("groups", "dp"), "seq", None),
        P(("groups", "dp"), "seq", None),
        P(("groups", "dp"), "seq", None),
        P(("groups", "dp"), "seq", None),
        P(("groups", "dp")),
        P(),
        P(),
        P("seq", None),
    )
    out_specs = (
        P(("groups", "dp"), "seq", None),
        P(("groups", "dp"), "seq", None),
        P(("groups", "dp"), "seq", None),
        P(("groups", "seq"), None),
        P("groups", None, "seq"),
        P(("groups", "seq")),
    )
    def chosen(query_proj, *rest):
        pairs, tok, _ = query_proj.shape
        dense = pairs == 1 and mesh.shape["dp"] == 2 and tok * mesh.shape["seq"] <= DENSE_LIMIT
        return (dense_body if dense else body)(query_proj, *rest)

    return jax.shard_map(chosen, mesh=mesh, in_specs=in_specs, out_specs=out_specs, check_vma=False)
```

```python
import functools
import math

import jax
import jax.numpy as jnp
import numpy as np
from jax import lax
from jax.experimental import pallas as pl
from jax.experimental.pallas import tpu as pltpu
from jax.sharding import PartitionSpec as P

DENSE_LIMIT = 1024
LANES = 128
MESH = pl.DeviceIdType.MESH


def passed_along(value, axis, by):
    count = lax.axis_size(axis)
    pairs = [(i, i + by) for i in range(count) if 0 <= i + by < count]
    return lax.ppermute(value, axis, pairs)


def matmul_high(form, left, right):
    return jnp.einsum(
        form, left, right, precision=lax.Precision.HIGHEST, preferred_element_type=jnp.float32
    )


def dot_high(left, right):
    return jnp.dot(left, right, precision=lax.Precision.HIGHEST, preferred_element_type=jnp.float32)


def angle_table(left, right, period):
    phase = (left[:, None] * right[None, :] % period).astype(jnp.float32) * (2.0 * math.pi / period)
    return (jnp.cos(phase), jnp.sin(phase))


def build_tables(seq_len):
    cols = min(128, seq_len)
    rows = 2 * seq_len // cols
    half = rows // 2
    keep = half + 1
    col_index = jnp.arange(cols, dtype=jnp.int32)
    keep_index = jnp.arange(keep, dtype=jnp.int32)
    half_index = jnp.arange(half, dtype=jnp.int32)
    col_cos, col_sin = angle_table(col_index, col_index, cols)
    first_cos, first_sin = angle_table(keep_index, half_index, rows)
    first = jnp.stack((first_cos, -first_sin))
    twist_cos, twist_sin = angle_table(keep_index, col_index, 2 * seq_len)
    twist_cos = twist_cos[:, None, :]
    twist_sin = twist_sin[:, None, :]
    fwd_real = jnp.concatenate((col_cos, -col_sin), axis=1)
    fwd_imag = jnp.concatenate((col_sin, col_cos), axis=1)
    inv_real = jnp.concatenate((col_cos, col_sin), axis=1)
    inv_imag = jnp.concatenate((-col_sin, col_cos), axis=1)
    edge = (keep_index == 0) | (keep_index == half)
    weights = jnp.where(edge, 1.0, 2.0).astype(jnp.float32) / (2.0 * seq_len)
    last_cos, last_sin = angle_table(half_index, keep_index, rows)
    last_cos = last_cos * weights[None, :]
    last_sin = last_sin * weights[None, :]
    return (first, twist_cos, twist_sin, fwd_real, fwd_imag, inv_real, inv_imag, last_cos, last_sin)


def forward_half(signal, tables):
    first, twist_cos, twist_sin, fwd_real, fwd_imag = tables[:5]
    width_c, length = signal.shape
    cols = fwd_real.shape[0]
    grid = jnp.transpose(signal.reshape(width_c, length // cols, cols), (1, 0, 2))
    partial_dft = matmul_high("pkn,nca->pkca", first, grid)
    turned_re = partial_dft[0] * twist_cos + partial_dft[1] * twist_sin
    turned_im = partial_dft[1] * twist_cos - partial_dft[0] * twist_sin
    keep = partial_dft.shape[1]
    spec = dot_high(turned_re.reshape(-1, cols), fwd_real) + dot_high(
        turned_im.reshape(-1, cols), fwd_imag
    )
    spec = spec.reshape(keep, width_c, 2, cols)
    return (spec[:, :, 0], spec[:, :, 1])


def inverse_half(spec_re, spec_im, tables):
    twist_cos, twist_sin = (tables[1], tables[2])
    inv_real, inv_imag, last_cos, last_sin = tables[5:]
    keep, width_c, cols = spec_re.shape
    wide = dot_high(spec_re.reshape(-1, cols), inv_real) + dot_high(
        spec_im.reshape(-1, cols), inv_imag
    )
    wide = wide.reshape(keep, width_c, 2, cols)
    wide_re = wide[:, :, 0]
    wide_im = wide[:, :, 1]
    turned_re = wide_re * twist_cos - wide_im * twist_sin
    turned_im = wide_im * twist_cos + wide_re * twist_sin
    grid = matmul_high("nk,kca->nca", last_cos, turned_re) - matmul_high(
        "nk,kca->nca", last_sin, turned_im
    )
    return jnp.transpose(grid, (1, 0, 2)).reshape(width_c, -1)


def convolve_cols(gated_spec, filt_spec, tables):
    gated_re, gated_im = gated_spec
    filt_re, filt_im = filt_spec
    return inverse_half(
        gated_re * filt_re - gated_im * filt_im, gated_re * filt_im + gated_im * filt_re, tables
    )


def correlate_cols(gated_spec, filt_spec, dmix_cols, tables):
    gated_re, gated_im = gated_spec
    filt_re, filt_im = filt_spec
    grad_re, grad_im = forward_half(dmix_cols, tables)
    back = inverse_half(
        filt_re * grad_re + filt_im * grad_im, filt_re * grad_im - filt_im * grad_re, tables
    )
    filt_part = inverse_half(
        grad_re * gated_re + grad_im * gated_im, grad_im * gated_re - grad_re * gated_im, tables
    )
    return (back, filt_part)


def phase_tables(n):
    index = 4 * np.arange(n, dtype=np.int64) + 1
    unit = 2.0 * np.pi / (16 * n)
    fine = (index[:, None] * index[None, :LANES] % (16 * n)) * unit
    coarse = (index[:, None] * (4 * LANES * np.arange(n // LANES))[None, :] % (16 * n)) * unit
    turn = index[:, None] * unit
    pack = lambda x: np.stack((np.cos(x), np.sin(x))).astype(np.float32)
    return pack(fine), pack(np.concatenate((coarse, turn), axis=1))


def split_to(ref, lead, rows, value, cols=slice(None)):
    high = value.astype(jnp.bfloat16)
    ref[(*lead, 0, rows, cols)] = high
    ref[(*lead, 1, rows, cols)] = (value - high.astype(jnp.float32)).astype(jnp.bfloat16)


def dot(left, right):
    return jnp.dot(left, right, preferred_element_type=jnp.float32)


def dot3(high, low, ref, lead):
    top = ref[(*lead, 0)]
    return dot(high, top) + (dot(high, ref[(*lead, 1)]) + dot(low, top))


def operator_kernel(
    n, parts, scale, bound, q_in, k_in, v_in, c_in, h_in, taps_in, skip_in, fine, coarse,
    gq_out, gk_out, gv_out, f_out, taps_out, skip_out,
    bufs, cosines, sines, gd, spec, hspec, gspec, s1s, s2s, dms, ds, filt, fother, fown, stage,
    taps, sums, sother, tsum, send_sem, recv_sem, local_sem, dp_send, dp_recv,
):
    tok = n // parts
    width = bufs.shape[2]
    half = width // 2
    rows = 64
    block = min(256, n)
    me = lax.axis_index("seq")
    core = lax.axis_index("dp")
    partner = {"dp": 1 - core}
    f32, bf16 = jnp.float32, jnp.bfloat16
    mine = pl.ds(pl.multiple_of(me * tok, tok), tok)
    my_half = pl.ds(pl.multiple_of(core * half, half), half)
    other_half = pl.ds(pl.multiple_of((1 - core) * half, half), half)

    def cols_of(owner):
        return pl.ds(pl.multiple_of(owner * width, width), width)

    def half_cols_of(owner):
        return pl.ds(pl.multiple_of(owner * width + core * half, half), half)

    peers = [lax.rem(me + s, parts) for s in range(parts)]

    barrier = pltpu.get_barrier_semaphore()
    for s in range(1, parts):
        pl.semaphore_signal(barrier, inc=1, device_id={"seq": peers[s]}, device_id_type=MESH)
    pl.semaphore_signal(barrier, inc=1, device_id=partner, device_id_type=MESH)
    pl.semaphore_wait(barrier, parts)

    def exchange(a, source, target):
        own = pltpu.make_async_copy(source(me), target, local_sem.at[a])
        own.start()
        copies = []
        for s in range(1, parts):
            copy = pltpu.make_async_remote_copy(
                src_ref=source(peers[s]),
                dst_ref=target,
                send_sem=send_sem.at[a, s],
                recv_sem=recv_sem.at[a, s],
                device_id={"seq": peers[s]},
                device_id_type=MESH,
            )
            copy.start()
            copies.append(copy)
        return own, copies

    def arrived(moved):
        moved[0].wait()
        for copy in moved[1]:
            copy.wait_recv()

    def to_partner(i, source, target):
        return pltpu.make_async_remote_copy(
            src_ref=source,
            dst_ref=target,
            send_sem=dp_send.at[i],
            recv_sem=dp_recv.at[i],
            device_id=partner,
            device_id_type=MESH,
        )

    hb, kb, vb, qb, cb = (bufs.at[i] for i in range(5))
    h_moved = exchange(0, lambda o: h_in.at[:, half_cols_of(o)], hb.at[mine, my_half])
    ins = [
        exchange(1 + i, lambda o, x=x: x.at[0, :, cols_of(o)], bufs.at[1 + i, mine, :])
        for i, x in enumerate((k_in, v_in, q_in, c_in))
    ]

    own_cols = cols_of(me)
    for b in range(3):
        taps[pl.ds(3 * b, 3), :] = taps_in[b, :, own_cols]
    taps[pl.ds(9, 1), :] = skip_in[:, own_cols]
    tsum[...] = jnp.zeros_like(tsum)
    ds[:, pl.ds(n, 8), :] = jnp.zeros((3, 8, width), f32)

    @pl.loop(0, n // rows)
    def _(i):
        at = pl.ds(pl.multiple_of(i * rows, rows), rows)
        fr, fi = fine[0, at, :], fine[1, at, :]
        cr, ci = coarse[0, at, :], coarse[1, at, :]
        for a in range(n // LANES):
            ar, ai = cr[:, a : a + 1], ci[:, a : a + 1]
            cols = slice(a * LANES, (a + 1) * LANES)
            split_to(cosines, (), at, fr * ar - fi * ai, cols)
            split_to(sines, (), at, fr * ai + fi * ar, cols)

    def tap(b, j):
        return taps[pl.ds(3 * b + j, 1), :]

    def gain():
        return taps[pl.ds(9, 1), :]

    def at_rows(i):
        return pl.ds(pl.multiple_of(i * rows, rows), rows)

    def lagged(ref, i):
        head = pl.multiple_of(jnp.maximum(i * rows - 16, 0), 16)
        halo = jnp.where(i > 0, ref[pl.ds(head, 16), :].astype(f32), 0.0)
        ext = jnp.concatenate((halo, ref[at_rows(i), :].astype(f32)), axis=0)
        return ext[16:], pltpu.roll(ext, 1, 0)[16:], pltpu.roll(ext, 2, 0)[16:]

    def short(b, lags):
        return tap(b, 0) * lags[0] + tap(b, 1) * lags[1] + tap(b, 2) * lags[2]

    def add_sum(i, value):
        tsum[i] += jnp.sum(value.reshape(rows // 8, 8, width), axis=0)

    def add_taps(b, d, lags):
        for j in range(3):
            add_sum(3 * b + j, d * lags[j])

    def short_back(b):
        @pl.loop(0, n // rows)
        def _(i):
            ext = ds[b, pl.ds(pl.multiple_of(i * rows, rows), rows + 8), :]
            g = tap(b, 0) * ext + tap(b, 1) * pltpu.roll(ext, rows + 7, 0)
            g = g + tap(b, 2) * pltpu.roll(ext, rows + 6, 0)
            stage[b, at_rows(i), :] = g[:rows].astype(bf16)

    def blocks(table, at):
        return table[0, at, :], table[1, at, :]

    def inverse(b, at):
        ch, cl = blocks(cosines, at)
        sh, sl = blocks(sines, at)
        return dot3(ch, cl, spec, (b, 0)) - dot3(sh, sl, spec, (b, 1))

    def turned(at, re, im):
        last = coarse.shape[2] - 1
        tr, ti = coarse[0, at, last:], coarse[1, at, last:]
        return re * tr - im * ti, re * ti + im * tr

    def at_block(j):
        return pl.ds(pl.multiple_of(j * block, block), block)

    arrived(h_moved)
    h_relay = to_partner(0, hb.at[:, my_half], hb.at[:, my_half])
    h_relay.start()
    arrived(ins[0])
    arrived(ins[1])

    @pl.loop(0, n // rows)
    def _(i):
        at = at_rows(i)
        s1 = short(1, lagged(kb, i))
        s2 = short(2, lagged(vb, i))
        s1s[at, :] = s1
        s2s[at, :] = s2
        split_to(gd, (0,), at, s1 * s2)

    h_relay.wait_recv()

    @pl.loop(0, n // block)
    def _(j):
        at = at_block(j)
        ch, cl = blocks(cosines, at)
        sh, sl = blocks(sines, at)
        h = hb[...]
        hr, hi = turned(at, dot(ch, h) + dot(cl, h), -(dot(sh, h) + dot(sl, h)))
        hspec[0, at, :], hspec[1, at, :] = hr, hi
        gr, gi = dot3(ch, cl, gd, (0,)), -dot3(sh, sl, gd, (0,))
        split_to(spec, (0, 0), at, gr * hr - gi * hi)
        split_to(spec, (0, 1), at, gr * hi + gi * hr)
        gspec[0, at, :], gspec[1, at, :] = turned(at, gr, gi)

    @pl.loop(0, n // block)
    def _(j):
        at = at_block(j)
        ds[0, at, :] = inverse(0, at) * (1.0 / n)

    arrived(ins[2])
    arrived(ins[3])

    @pl.loop(0, n // rows)
    def _(i):
        at = at_rows(i)
        pos = i * rows + lax.broadcasted_iota(jnp.int32, (rows, width), 0)
        dout = jnp.where(pos >= bound[0], cb[at, :].astype(f32), 0.0)
        gated = s1s[at, :] * s2s[at, :]
        lags = lagged(qb, i)
        dmix = dout * short(0, lags)
        d = dout * (ds[0, at, :] + gain() * gated)
        ds[0, at, :] = d
        dms[at, :] = dmix
        split_to(gd, (1,), at, dmix)
        add_sum(9, dmix * gated)
        add_taps(0, d, lags)

    def send_back(b, out):
        short_back(b)
        return exchange(5 + b, lambda o: stage.at[b, rows_of(o), :], out.at[0, :, own_cols])

    def rows_of(owner):
        return pl.ds(pl.multiple_of(owner * tok, tok), tok)

    gq_moved = send_back(0, gq_out)

    @pl.loop(0, n // block)
    def _(j):
        at = at_block(j)
        ch, cl = blocks(cosines, at)
        sh, sl = blocks(sines, at)
        dr, di = dot3(ch, cl, gd, (1,)), -dot3(sh, sl, gd, (1,))
        hr, hi = hspec[0, at, :], hspec[1, at, :]
        split_to(spec, (1, 0), at, hr * dr + hi * di)
        split_to(spec, (1, 1), at, hr * di - hi * dr)
        gr, gi = gspec[0, at, :], gspec[1, at, :]
        split_to(spec, (2, 0), at, gr * dr + gi * di)
        split_to(spec, (2, 1), at, gr * di - gi * dr)

    @pl.loop(0, n // block)
    def _(j):
        at = at_block(j)
        ds[1, at, :] = inverse(1, at) * (1.0 / n)

    @pl.loop(0, n // rows)
    def _(i):
        at = at_rows(i)
        dg = ds[1, at, :] + gain() * dms[at, :]
        for b, other, ref in ((1, s2s, kb), (2, s1s, vb)):
            d = dg * other[at, :]
            ds[b, at, :] = d
            add_taps(b, d, lagged(ref, i))

    gk_moved = send_back(1, gk_out)
    gv_moved = send_back(2, gv_out)

    @pl.loop(0, n // block)
    def _(j):
        at = at_block(j)
        filt[at, :] = inverse(2, at) * (scale / n)

    f_add = to_partner(1, filt.at[:, other_half], fother)
    f_add.start()
    sums[...] = jnp.zeros_like(sums)
    sums[pl.ds(0, 10), :] = jnp.sum(tsum[...], axis=1) * scale
    s_add = to_partner(2, sums, sother)
    s_add.start()
    f_add.wait_recv()

    @pl.loop(0, n // rows)
    def _(i):
        at = at_rows(i)
        fown[at, :] = (filt[at, my_half] + fother[at, :]).astype(bf16)

    f_moved = exchange(8, lambda o: fown.at[rows_of(o), :], f_out.at[:, half_cols_of(me)])
    own_relay = to_partner(3, fown.at[mine, :], f_out.at[:, half_cols_of(me)])
    own_relay.start()
    s_add.wait_recv()
    total = sums[...] + sother[...]
    for b in range(3):
        taps_out[b] = total[3 * b : 3 * b + 3]
    skip_out[...] = total[9:10]

    relays = [own_relay]
    for s in range(1, parts):
        f_moved[1][s - 1].wait_recv()
        block_cols = half_cols_of(lax.rem(me + parts - s, parts))
        relay = to_partner(3 + s, f_out.at[:, block_cols], f_out.at[:, block_cols])
        relay.start()
        relays.append(relay)
    f_moved[0].wait()
    for moved in (gq_moved, gk_moved, gv_moved):
        arrived(moved)
    for relay in relays:
        relay.wait_recv()
    for moved in (h_moved, *ins, gq_moved, gk_moved, gv_moved, f_moved):
        for copy in moved[1]:
            copy.wait_send()
    for copy in (h_relay, f_add, s_add, *relays):
        copy.wait_send()


def copy_kernel(*refs):
    count = len(refs) // 2
    copies = [
        pltpu.make_async_copy(refs[i], refs[count + i], refs[-1].at[i]) for i in range(count)
    ]
    for copy in copies:
        copy.start()
    for copy in copies:
        copy.wait()


def dense_body(query_proj, key_proj, value_proj, cotangent, boundary, short_taps, skip_gain, long_filter):
    tok, width = query_proj.shape[1:]
    parts = lax.axis_size("seq")
    n = tok * parts
    own = width // parts
    scale = 1.0 / math.sqrt(lax.axis_size("dp") * n)
    fine, coarse = phase_tables(n)
    vmem = pl.BlockSpec(memory_space=pltpu.VMEM)
    anywhere = pl.BlockSpec(memory_space=pl.ANY)
    f32, bf16 = jnp.float32, jnp.bfloat16
    shape = jax.ShapeDtypeStruct
    dma = pltpu.SemaphoreType.DMA
    results = pl.pallas_call(
        functools.partial(operator_kernel, n, parts, scale),
        out_shape=[shape((1, tok, width), bf16)] * 3
        + [shape((tok, width), bf16), shape((3, 3, own), f32), shape((1, own), f32)],
        in_specs=[pl.BlockSpec(memory_space=pltpu.SMEM)] + [anywhere] * 5 + [vmem] * 4,
        out_specs=[anywhere] * 4 + [vmem] * 2,
        scratch_shapes=[
            pltpu.VMEM((5, n, own), bf16),
            pltpu.VMEM((2, n, n), bf16),
            pltpu.VMEM((2, n, n), bf16),
            pltpu.VMEM((2, 2, n, own), bf16),
            pltpu.VMEM((3, 2, 2, n, own), bf16),
            pltpu.VMEM((2, n, own), f32),
            pltpu.VMEM((2, n, own), f32),
            pltpu.VMEM((n, own), f32),
            pltpu.VMEM((n, own), f32),
            pltpu.VMEM((n, own), f32),
            pltpu.VMEM((3, n + 8, own), f32),
            pltpu.VMEM((n, own), f32),
            pltpu.VMEM((n, own // 2), f32),
            pltpu.VMEM((n, own // 2), bf16),
            pltpu.VMEM((3, n, own), bf16),
            pltpu.VMEM((16, own), f32),
            pltpu.VMEM((16, own), f32),
            pltpu.VMEM((16, own), f32),
            pltpu.VMEM((10, 8, own), f32),
            dma((9, parts)),
            dma((9, parts)),
            dma((9,)),
            dma((3 + parts,)),
            dma((3 + parts,)),
        ],
        compiler_params=pltpu.CompilerParams(
            collective_id=0, has_side_effects=True, vmem_limit_bytes=56 * 2**20
        ),
    )(
        boundary, query_proj, key_proj, value_proj, cotangent, long_filter,
        short_taps, skip_gain[None], jnp.asarray(fine), jnp.asarray(coarse),
    )
    gq, gk, gv, filter_grad, taps_grad, skip_grad = pl.pallas_call(
        copy_kernel,
        out_shape=[shape(x.shape, x.dtype) for x in results],
        in_specs=[anywhere] * len(results),
        out_specs=[anywhere] * len(results),
        scratch_shapes=[dma((len(results),))],
    )(*results)
    return gq, gk, gv, filter_grad, taps_grad, skip_grad.reshape(own)


def body(query_proj, key_proj, value_proj, cotangent, boundary, short_taps, skip_gain, long_filter):
    pairs, tok, width = query_proj.shape
    parts = lax.axis_size("seq")
    seq_len = tok * parts
    scale = 1.0 / math.sqrt(pairs * lax.axis_size("dp") * seq_len)
    tables = build_tables(seq_len)
    filter_cols = lax.all_to_all(
        jnp.transpose(long_filter), "seq", split_axis=0, concat_axis=1, tiled=True
    ).astype(jnp.float32)
    filt_spec = forward_half(filter_cols, tables)
    taps = short_taps[:, :, None, None, :]
    raw = jnp.stack((query_proj, key_proj, value_proj))
    tails = passed_along(raw[:, :, tok - 2 :], "seq", 1)
    extended = jnp.concatenate((tails, raw), axis=2).astype(jnp.float32)
    conv = (
        taps[:, 0] * extended[:, :, 2:]
        + taps[:, 1] * extended[:, :, 1:-1]
        + taps[:, 2] * extended[:, :, :-2]
    )
    gated = conv[1] * conv[2]
    position = lax.axis_index("seq") * tok + jnp.arange(tok, dtype=jnp.int32)
    mask = (position[None, :] >= boundary[:, None]).astype(jnp.float32)
    dout = cotangent.astype(jnp.float32) * mask[:, :, None]
    dmix = dout * conv[0]
    gated_cols = lax.all_to_all(
        jnp.transpose(gated, (0, 2, 1)), "seq", split_axis=1, concat_axis=2, tiled=True
    )
    spectra = forward_half(gated_cols[0], tables)
    conv_cols = jnp.stack([convolve_cols(spectra, filt_spec, tables)])
    conv_rows = lax.all_to_all(conv_cols, "seq", split_axis=2, concat_axis=1, tiled=True)
    dmix_cols = lax.all_to_all(
        jnp.transpose(dmix, (0, 2, 1)), "seq", split_axis=1, concat_axis=2, tiled=True
    )
    back_cols, filt_part = correlate_cols(spectra, filt_spec, dmix_cols[0], tables)
    back_list = [back_cols]
    filt_list = [filt_part]
    back_rows = lax.all_to_all(jnp.stack(back_list), "seq", split_axis=2, concat_axis=1, tiled=True)
    mixed = jnp.transpose(conv_rows, (0, 2, 1)) + skip_gain * gated
    filter_part = jnp.sum(jnp.stack(filt_list), axis=0) * scale
    filter_total = lax.psum(filter_part, "dp")
    filter_rows = lax.all_to_all(
        filter_total.astype(jnp.bfloat16), "seq", split_axis=1, concat_axis=0, tiled=True
    )
    filter_grad = jnp.transpose(filter_rows)
    dgated = jnp.transpose(back_rows, (0, 2, 1)) + skip_gain * dmix
    upstream = jnp.stack((dout * mixed, dgated * conv[2], dgated * conv[1]))
    heads = passed_along(upstream[:, :, :2], "seq", -1)
    grad_ext = jnp.concatenate((upstream, heads), axis=2)
    grads = (
        taps[:, 0] * grad_ext[:, :, :tok]
        + taps[:, 1] * grad_ext[:, :, 1 : tok + 1]
        + taps[:, 2] * grad_ext[:, :, 2:]
    )
    grads = grads.astype(jnp.bfloat16)
    taps_part = (
        jnp.stack(
            [
                jnp.sum(upstream * extended[:, :, 2 - lag : 2 - lag + tok], axis=(1, 2))
                for lag in range(3)
            ],
            axis=1,
        )
        * scale
    )
    skip_part = jnp.sum(dmix * gated, axis=(0, 1)) * scale
    taps_local, skip_local = (
        lax.psum_scatter(taps_part, "seq", scatter_dimension=2, tiled=True),
        lax.psum_scatter(skip_part, "seq", scatter_dimension=0, tiled=True),
    )
    taps_grad, skip_grad = lax.psum((taps_local, skip_local), "dp")
    return (grads[0], grads[1], grads[2], filter_grad, taps_grad, skip_grad)


def solution(mesh):
    in_specs = (
        P(("groups", "dp"), "seq", None),
        P(("groups", "dp"), "seq", None),
        P(("groups", "dp"), "seq", None),
        P(("groups", "dp"), "seq", None),
        P(("groups", "dp")),
        P(),
        P(),
        P("seq", None),
    )
    out_specs = (
        P(("groups", "dp"), "seq", None),
        P(("groups", "dp"), "seq", None),
        P(("groups", "dp"), "seq", None),
        P(("groups", "seq"), None),
        P("groups", None, "seq"),
        P(("groups", "seq")),
    )
    def chosen(query_proj, *rest):
        pairs, tok, _ = query_proj.shape
        dense = pairs == 1 and mesh.shape["dp"] == 2 and tok * mesh.shape["seq"] <= DENSE_LIMIT
        return (dense_body if dense else body)(query_proj, *rest)

    return jax.shard_map(chosen, mesh=mesh, in_specs=in_specs, out_specs=out_specs, check_vma=False)
```

```python
import functools
import math

import jax
import jax.numpy as jnp
import numpy as np
from jax import lax
from jax.experimental import pallas as pl
from jax.experimental.pallas import tpu as pltpu
from jax.sharding import PartitionSpec as P

DENSE_LIMIT = 1024
LANES = 128
MESH = pl.DeviceIdType.MESH


def passed_along(value, axis, by):
    count = lax.axis_size(axis)
    pairs = [(i, i + by) for i in range(count) if 0 <= i + by < count]
    return lax.ppermute(value, axis, pairs)


def matmul_high(form, left, right):
    return jnp.einsum(
        form, left, right, precision=lax.Precision.HIGHEST, preferred_element_type=jnp.float32
    )


def dot_high(left, right):
    return jnp.dot(left, right, precision=lax.Precision.HIGHEST, preferred_element_type=jnp.float32)


def angle_table(left, right, period):
    phase = (left[:, None] * right[None, :] % period).astype(jnp.float32) * (2.0 * math.pi / period)
    return (jnp.cos(phase), jnp.sin(phase))


def build_tables(seq_len):
    cols = min(128, seq_len)
    rows = 2 * seq_len // cols
    half = rows // 2
    keep = half + 1
    col_index = jnp.arange(cols, dtype=jnp.int32)
    keep_index = jnp.arange(keep, dtype=jnp.int32)
    half_index = jnp.arange(half, dtype=jnp.int32)
    col_cos, col_sin = angle_table(col_index, col_index, cols)
    first_cos, first_sin = angle_table(keep_index, half_index, rows)
    first = jnp.stack((first_cos, -first_sin))
    twist_cos, twist_sin = angle_table(keep_index, col_index, 2 * seq_len)
    twist_cos = twist_cos[:, None, :]
    twist_sin = twist_sin[:, None, :]
    fwd_real = jnp.concatenate((col_cos, -col_sin), axis=1)
    fwd_imag = jnp.concatenate((col_sin, col_cos), axis=1)
    inv_real = jnp.concatenate((col_cos, col_sin), axis=1)
    inv_imag = jnp.concatenate((-col_sin, col_cos), axis=1)
    edge = (keep_index == 0) | (keep_index == half)
    weights = jnp.where(edge, 1.0, 2.0).astype(jnp.float32) / (2.0 * seq_len)
    last_cos, last_sin = angle_table(half_index, keep_index, rows)
    last_cos = last_cos * weights[None, :]
    last_sin = last_sin * weights[None, :]
    return (first, twist_cos, twist_sin, fwd_real, fwd_imag, inv_real, inv_imag, last_cos, last_sin)


def forward_half(signal, tables):
    first, twist_cos, twist_sin, fwd_real, fwd_imag = tables[:5]
    width_c, length = signal.shape
    cols = fwd_real.shape[0]
    grid = jnp.transpose(signal.reshape(width_c, length // cols, cols), (1, 0, 2))
    partial_dft = matmul_high("pkn,nca->pkca", first, grid)
    turned_re = partial_dft[0] * twist_cos + partial_dft[1] * twist_sin
    turned_im = partial_dft[1] * twist_cos - partial_dft[0] * twist_sin
    keep = partial_dft.shape[1]
    spec = dot_high(turned_re.reshape(-1, cols), fwd_real) + dot_high(
        turned_im.reshape(-1, cols), fwd_imag
    )
    spec = spec.reshape(keep, width_c, 2, cols)
    return (spec[:, :, 0], spec[:, :, 1])


def inverse_half(spec_re, spec_im, tables):
    twist_cos, twist_sin = (tables[1], tables[2])
    inv_real, inv_imag, last_cos, last_sin = tables[5:]
    keep, width_c, cols = spec_re.shape
    wide = dot_high(spec_re.reshape(-1, cols), inv_real) + dot_high(
        spec_im.reshape(-1, cols), inv_imag
    )
    wide = wide.reshape(keep, width_c, 2, cols)
    wide_re = wide[:, :, 0]
    wide_im = wide[:, :, 1]
    turned_re = wide_re * twist_cos - wide_im * twist_sin
    turned_im = wide_im * twist_cos + wide_re * twist_sin
    grid = matmul_high("nk,kca->nca", last_cos, turned_re) - matmul_high(
        "nk,kca->nca", last_sin, turned_im
    )
    return jnp.transpose(grid, (1, 0, 2)).reshape(width_c, -1)


def convolve_cols(gated_spec, filt_spec, tables):
    gated_re, gated_im = gated_spec
    filt_re, filt_im = filt_spec
    return inverse_half(
        gated_re * filt_re - gated_im * filt_im, gated_re * filt_im + gated_im * filt_re, tables
    )


def correlate_cols(gated_spec, filt_spec, dmix_cols, tables):
    gated_re, gated_im = gated_spec
    filt_re, filt_im = filt_spec
    grad_re, grad_im = forward_half(dmix_cols, tables)
    back = inverse_half(
        filt_re * grad_re + filt_im * grad_im, filt_re * grad_im - filt_im * grad_re, tables
    )
    filt_part = inverse_half(
        grad_re * gated_re + grad_im * gated_im, grad_im * gated_re - grad_re * gated_im, tables
    )
    return (back, filt_part)


def phase_tables(n):
    index = 4 * np.arange(n, dtype=np.int64) + 1
    unit = 2.0 * np.pi / (16 * n)
    fine = (index[:, None] * index[None, :LANES] % (16 * n)) * unit
    coarse = (index[:, None] * (4 * LANES * np.arange(n // LANES))[None, :] % (16 * n)) * unit
    turn = index[:, None] * unit
    pack = lambda x: np.stack((np.cos(x), np.sin(x))).astype(np.float32)
    return pack(fine), pack(np.concatenate((coarse, turn), axis=1))


def split_to(ref, lead, rows, value, cols=slice(None)):
    high = value.astype(jnp.bfloat16)
    ref[(*lead, 0, rows, cols)] = high
    ref[(*lead, 1, rows, cols)] = (value - high.astype(jnp.float32)).astype(jnp.bfloat16)


def dot(left, right):
    return jnp.dot(left, right, preferred_element_type=jnp.float32)


def dot3(high, low, ref, lead):
    top = ref[(*lead, 0)]
    return dot(high, top) + (dot(high, ref[(*lead, 1)]) + dot(low, top))


def operator_kernel(
    n, parts, scale, bound, q_in, k_in, v_in, c_in, h_in, taps_in, skip_in, fine, coarse,
    gq_out, gk_out, gv_out, f_out, taps_out, skip_out,
    hb, bufs, cosines, sines, gd, spec, hspec, gspec, s1s, s2s, dms, ds, filt, fother, fown, stage,
    taps, sums, sother, tsum, send_sem, recv_sem, local_sem, dp_send, dp_recv,
):
    tok = n // parts
    width = bufs.shape[2]
    half = width // 2
    rows = 64
    block = min(256, n)
    me = lax.axis_index("seq")
    core = lax.axis_index("dp")
    group = lax.axis_index("groups")
    partner = {"dp": 1 - core}
    twin = {"groups": 1 - group}
    group_rows = pl.ds(pl.multiple_of(group * (tok // 2), tok // 2), tok // 2)
    f32, bf16 = jnp.float32, jnp.bfloat16
    mine = pl.ds(pl.multiple_of(me * tok, tok), tok)
    my_half = pl.ds(pl.multiple_of(core * half, half), half)
    other_half = pl.ds(pl.multiple_of((1 - core) * half, half), half)

    def cols_of(owner):
        return pl.ds(pl.multiple_of(owner * width, width), width)

    def half_cols_of(owner):
        return pl.ds(pl.multiple_of(owner * width + core * half, half), half)

    peers = [lax.rem(me + s, parts) for s in range(parts)]

    barrier = pltpu.get_barrier_semaphore()
    for s in range(1, parts):
        pl.semaphore_signal(barrier, inc=1, device_id={"seq": peers[s]}, device_id_type=MESH)
    for other in (partner, twin):
        pl.semaphore_signal(barrier, inc=1, device_id=other, device_id_type=MESH)
    pl.semaphore_wait(barrier, parts + 1)

    def exchange(a, source, target):
        own = pltpu.make_async_copy(source(me), target, local_sem.at[a])
        own.start()
        copies = []
        for s in range(1, parts):
            copy = pltpu.make_async_remote_copy(
                src_ref=source(peers[s]),
                dst_ref=target,
                send_sem=send_sem.at[a, s],
                recv_sem=recv_sem.at[a, s],
                device_id={"seq": peers[s]},
                device_id_type=MESH,
            )
            copy.start()
            copies.append(copy)
        return own, copies

    def arrived(moved):
        moved[0].wait()
        for copy in moved[1]:
            copy.wait_recv()

    def to_partner(i, source, target, device=partner):
        return pltpu.make_async_remote_copy(
            src_ref=source,
            dst_ref=target,
            send_sem=dp_send.at[i],
            recv_sem=dp_recv.at[i],
            device_id=device,
            device_id_type=MESH,
        )

    kb, vb, qb, cb = (bufs.at[i] for i in range(4))
    h_moved = exchange(
        0, lambda o: h_in.at[group_rows, half_cols_of(o)], hb.at[me, group, :, my_half]
    )
    ins = [
        exchange(1 + i, lambda o, x=x: x.at[0, :, cols_of(o)], bufs.at[i, mine, :])
        for i, x in enumerate((k_in, v_in, q_in, c_in))
    ]

    own_cols = cols_of(me)
    for b in range(3):
        taps[pl.ds(3 * b, 3), :] = taps_in[b, :, own_cols]
    taps[pl.ds(9, 1), :] = skip_in[:, own_cols]
    tsum[...] = jnp.zeros_like(tsum)
    ds[:, pl.ds(n, 8), :] = jnp.zeros((3, 8, width), f32)

    @pl.loop(0, n // rows)
    def _(i):
        at = pl.ds(pl.multiple_of(i * rows, rows), rows)
        fr, fi = fine[0, at, :], fine[1, at, :]
        cr, ci = coarse[0, at, :], coarse[1, at, :]
        for a in range(n // LANES):
            ar, ai = cr[:, a : a + 1], ci[:, a : a + 1]
            cols = slice(a * LANES, (a + 1) * LANES)
            split_to(cosines, (), at, fr * ar - fi * ai, cols)
            split_to(sines, (), at, fr * ai + fi * ar, cols)

    def tap(b, j):
        return taps[pl.ds(3 * b + j, 1), :]

    def gain():
        return taps[pl.ds(9, 1), :]

    def at_rows(i):
        return pl.ds(pl.multiple_of(i * rows, rows), rows)

    def lagged(ref, i):
        head = pl.multiple_of(jnp.maximum(i * rows - 16, 0), 16)
        halo = jnp.where(i > 0, ref[pl.ds(head, 16), :].astype(f32), 0.0)
        ext = jnp.concatenate((halo, ref[at_rows(i), :].astype(f32)), axis=0)
        return ext[16:], pltpu.roll(ext, 1, 0)[16:], pltpu.roll(ext, 2, 0)[16:]

    def short(b, lags):
        return tap(b, 0) * lags[0] + tap(b, 1) * lags[1] + tap(b, 2) * lags[2]

    def add_sum(i, value):
        tsum[i] += jnp.sum(value.reshape(rows // 8, 8, width), axis=0)

    def add_taps(b, d, lags):
        for j in range(3):
            add_sum(3 * b + j, d * lags[j])

    def short_back(b):
        @pl.loop(0, n // rows)
        def _(i):
            ext = ds[b, pl.ds(pl.multiple_of(i * rows, rows), rows + 8), :]
            g = tap(b, 0) * ext + tap(b, 1) * pltpu.roll(ext, rows + 7, 0)
            g = g + tap(b, 2) * pltpu.roll(ext, rows + 6, 0)
            stage[b, at_rows(i), :] = g[:rows].astype(bf16)

    def blocks(table, at):
        return table[0, at, :], table[1, at, :]

    def inverse(b, at):
        ch, cl = blocks(cosines, at)
        sh, sl = blocks(sines, at)
        return dot3(ch, cl, spec, (b, 0)) - dot3(sh, sl, spec, (b, 1))

    def turned(at, re, im):
        last = coarse.shape[2] - 1
        tr, ti = coarse[0, at, last:], coarse[1, at, last:]
        return re * tr - im * ti, re * ti + im * tr

    def at_block(j):
        return pl.ds(pl.multiple_of(j * block, block), block)

    arrived(h_moved)
    h_quarter = hb.at[:, group, :, my_half]
    h_twin = to_partner(3 + parts, h_quarter, h_quarter, twin)
    h_twin.start()
    arrived(ins[0])
    h_twin.wait_recv()
    h_relay = to_partner(0, hb.at[:, :, :, my_half], hb.at[:, :, :, my_half])
    h_relay.start()
    arrived(ins[1])

    @pl.loop(0, n // rows)
    def _(i):
        at = at_rows(i)
        s1 = short(1, lagged(kb, i))
        s2 = short(2, lagged(vb, i))
        s1s[at, :] = s1
        s2s[at, :] = s2
        split_to(gd, (0,), at, s1 * s2)

    h_relay.wait_recv()

    @pl.loop(0, n // block)
    def _(j):
        at = at_block(j)
        ch, cl = blocks(cosines, at)
        sh, sl = blocks(sines, at)
        h = hb[...].reshape(n, width)
        hr, hi = turned(at, dot(ch, h) + dot(cl, h), -(dot(sh, h) + dot(sl, h)))
        hspec[0, at, :], hspec[1, at, :] = hr, hi
        gr, gi = dot3(ch, cl, gd, (0,)), -dot3(sh, sl, gd, (0,))
        split_to(spec, (0, 0), at, gr * hr - gi * hi)
        split_to(spec, (0, 1), at, gr * hi + gi * hr)
        gspec[0, at, :], gspec[1, at, :] = turned(at, gr, gi)

    @pl.loop(0, n // block)
    def _(j):
        at = at_block(j)
        ds[0, at, :] = inverse(0, at) * (1.0 / n)

    arrived(ins[2])
    arrived(ins[3])

    @pl.loop(0, n // rows)
    def _(i):
        at = at_rows(i)
        pos = i * rows + lax.broadcasted_iota(jnp.int32, (rows, width), 0)
        dout = jnp.where(pos >= bound[0], cb[at, :].astype(f32), 0.0)
        gated = s1s[at, :] * s2s[at, :]
        lags = lagged(qb, i)
        dmix = dout * short(0, lags)
        d = dout * (ds[0, at, :] + gain() * gated)
        ds[0, at, :] = d
        dms[at, :] = dmix
        split_to(gd, (1,), at, dmix)
        add_sum(9, dmix * gated)
        add_taps(0, d, lags)

    def send_back(b, out):
        short_back(b)
        return exchange(5 + b, lambda o: stage.at[b, rows_of(o), :], out.at[0, :, own_cols])

    def rows_of(owner):
        return pl.ds(pl.multiple_of(owner * tok, tok), tok)

    gq_moved = send_back(0, gq_out)

    @pl.loop(0, n // block)
    def _(j):
        at = at_block(j)
        ch, cl = blocks(cosines, at)
        sh, sl = blocks(sines, at)
        dr, di = dot3(ch, cl, gd, (1,)), -dot3(sh, sl, gd, (1,))
        hr, hi = hspec[0, at, :], hspec[1, at, :]
        split_to(spec, (1, 0), at, hr * dr + hi * di)
        split_to(spec, (1, 1), at, hr * di - hi * dr)
        gr, gi = gspec[0, at, :], gspec[1, at, :]
        split_to(spec, (2, 0), at, gr * dr + gi * di)
        split_to(spec, (2, 1), at, gr * di - gi * dr)

    @pl.loop(0, n // block)
    def _(j):
        at = at_block(j)
        filt[at, :] = inverse(2, at) * (scale / n)

    f_add = to_partner(1, filt.at[:, other_half], fother)
    f_add.start()
    f_add.wait_recv()

    @pl.loop(0, n // rows)
    def _(i):
        at = at_rows(i)
        fown[at, :] = (filt[at, my_half] + fother[at, :]).astype(bf16)

    f_moved = exchange(8, lambda o: fown.at[rows_of(o), :], f_out.at[:, half_cols_of(me)])
    own_relay = to_partner(3, fown.at[mine, :], f_out.at[:, half_cols_of(me)])
    own_relay.start()
    @pl.loop(0, n // block)
    def _(j):
        at = at_block(j)
        ds[1, at, :] = inverse(1, at) * (1.0 / n)

    @pl.loop(0, n // rows)
    def _(i):
        at = at_rows(i)
        dg = ds[1, at, :] + gain() * dms[at, :]
        for b, other, ref in ((1, s2s, kb), (2, s1s, vb)):
            d = dg * other[at, :]
            ds[b, at, :] = d
            add_taps(b, d, lagged(ref, i))

    gk_moved = send_back(1, gk_out)
    gv_moved = send_back(2, gv_out)

    sums[...] = jnp.zeros_like(sums)
    sums[pl.ds(0, 10), :] = jnp.sum(tsum[...], axis=1) * scale
    s_add = to_partner(2, sums, sother)
    s_add.start()
    s_add.wait_recv()
    total = sums[...] + sother[...]
    for b in range(3):
        taps_out[b] = total[3 * b : 3 * b + 3]
    skip_out[...] = total[9:10]

    relays = [own_relay]
    for s in range(1, parts):
        f_moved[1][s - 1].wait_recv()
        block_cols = half_cols_of(lax.rem(me + parts - s, parts))
        relay = to_partner(3 + s, f_out.at[:, block_cols], f_out.at[:, block_cols])
        relay.start()
        relays.append(relay)
    f_moved[0].wait()
    for moved in (gq_moved, gk_moved, gv_moved):
        arrived(moved)
    for relay in relays:
        relay.wait_recv()
    for moved in (h_moved, *ins, gq_moved, gk_moved, gv_moved, f_moved):
        for copy in moved[1]:
            copy.wait_send()
    for copy in (h_twin, h_relay, f_add, s_add, *relays):
        copy.wait_send()


def copy_kernel(*refs):
    count = len(refs) // 2
    for i in range(count):
        refs[count + i][...] = refs[i][...]


def dense_body(query_proj, key_proj, value_proj, cotangent, boundary, short_taps, skip_gain, long_filter):
    tok, width = query_proj.shape[1:]
    parts = lax.axis_size("seq")
    n = tok * parts
    own = width // parts
    scale = 1.0 / math.sqrt(lax.axis_size("dp") * n)
    fine, coarse = phase_tables(n)
    vmem = pl.BlockSpec(memory_space=pltpu.VMEM)
    anywhere = pl.BlockSpec(memory_space=pl.ANY)
    f32, bf16 = jnp.float32, jnp.bfloat16
    shape = jax.ShapeDtypeStruct
    dma = pltpu.SemaphoreType.DMA
    blocks = [pl.BlockSpec((1, tok // 4, width), lambda i: (0, i, 0))] * 3 + [
        pl.BlockSpec((tok // 4, width), lambda i: (i, 0)),
        pl.BlockSpec((3, 3, own), lambda i: (0, 0, 0)),
        pl.BlockSpec((1, own), lambda i: (0, 0)),
    ]
    results = pl.pallas_call(
        functools.partial(operator_kernel, n, parts, scale),
        out_shape=[shape((1, tok, width), bf16)] * 3
        + [shape((tok, width), bf16), shape((3, 3, own), f32), shape((1, own), f32)],
        in_specs=[pl.BlockSpec(memory_space=pltpu.SMEM)] + [anywhere] * 5 + [vmem] * 4,
        out_specs=[anywhere] * 4 + [vmem] * 2,
        scratch_shapes=[
            pltpu.VMEM((parts, 2, tok // 2, own), bf16),
            pltpu.VMEM((4, n, own), bf16),
            pltpu.VMEM((2, n, n), bf16),
            pltpu.VMEM((2, n, n), bf16),
            pltpu.VMEM((2, 2, n, own), bf16),
            pltpu.VMEM((3, 2, 2, n, own), bf16),
            pltpu.VMEM((2, n, own), f32),
            pltpu.VMEM((2, n, own), f32),
            pltpu.VMEM((n, own), f32),
            pltpu.VMEM((n, own), f32),
            pltpu.VMEM((n, own), f32),
            pltpu.VMEM((3, n + 8, own), f32),
            pltpu.VMEM((n, own), f32),
            pltpu.VMEM((n, own // 2), f32),
            pltpu.VMEM((n, own // 2), bf16),
            pltpu.VMEM((3, n, own), bf16),
            pltpu.VMEM((16, own), f32),
            pltpu.VMEM((16, own), f32),
            pltpu.VMEM((16, own), f32),
            pltpu.VMEM((10, 8, own), f32),
            dma((9, parts)),
            dma((9, parts)),
            dma((9,)),
            dma((4 + parts,)),
            dma((4 + parts,)),
        ],
        compiler_params=pltpu.CompilerParams(
            collective_id=0, has_side_effects=True, vmem_limit_bytes=56 * 2**20
        ),
    )(
        boundary, query_proj, key_proj, value_proj, cotangent, long_filter,
        short_taps, skip_gain[None], jnp.asarray(fine), jnp.asarray(coarse),
    )
    gq, gk, gv, filter_grad, taps_grad, skip_grad = pl.pallas_call(
        copy_kernel,
        out_shape=[shape(x.shape, x.dtype) for x in results],
        grid=(4,),
        in_specs=blocks,
        out_specs=blocks,
    )(*results)
    return gq, gk, gv, filter_grad, taps_grad, skip_grad.reshape(own)


def body(query_proj, key_proj, value_proj, cotangent, boundary, short_taps, skip_gain, long_filter):
    pairs, tok, width = query_proj.shape
    parts = lax.axis_size("seq")
    seq_len = tok * parts
    scale = 1.0 / math.sqrt(pairs * lax.axis_size("dp") * seq_len)
    tables = build_tables(seq_len)
    filter_cols = lax.all_to_all(
        jnp.transpose(long_filter), "seq", split_axis=0, concat_axis=1, tiled=True
    ).astype(jnp.float32)
    filt_spec = forward_half(filter_cols, tables)
    taps = short_taps[:, :, None, None, :]
    raw = jnp.stack((query_proj, key_proj, value_proj))
    tails = passed_along(raw[:, :, tok - 2 :], "seq", 1)
    extended = jnp.concatenate((tails, raw), axis=2).astype(jnp.float32)
    conv = (
        taps[:, 0] * extended[:, :, 2:]
        + taps[:, 1] * extended[:, :, 1:-1]
        + taps[:, 2] * extended[:, :, :-2]
    )
    gated = conv[1] * conv[2]
    position = lax.axis_index("seq") * tok + jnp.arange(tok, dtype=jnp.int32)
    mask = (position[None, :] >= boundary[:, None]).astype(jnp.float32)
    dout = cotangent.astype(jnp.float32) * mask[:, :, None]
    dmix = dout * conv[0]
    gated_cols = lax.all_to_all(
        jnp.transpose(gated, (0, 2, 1)), "seq", split_axis=1, concat_axis=2, tiled=True
    )
    spectra = forward_half(gated_cols[0], tables)
    conv_cols = jnp.stack([convolve_cols(spectra, filt_spec, tables)])
    conv_rows = lax.all_to_all(conv_cols, "seq", split_axis=2, concat_axis=1, tiled=True)
    dmix_cols = lax.all_to_all(
        jnp.transpose(dmix, (0, 2, 1)), "seq", split_axis=1, concat_axis=2, tiled=True
    )
    back_cols, filt_part = correlate_cols(spectra, filt_spec, dmix_cols[0], tables)
    back_list = [back_cols]
    filt_list = [filt_part]
    back_rows = lax.all_to_all(jnp.stack(back_list), "seq", split_axis=2, concat_axis=1, tiled=True)
    mixed = jnp.transpose(conv_rows, (0, 2, 1)) + skip_gain * gated
    filter_part = jnp.sum(jnp.stack(filt_list), axis=0) * scale
    filter_total = lax.psum(filter_part, "dp")
    filter_rows = lax.all_to_all(
        filter_total.astype(jnp.bfloat16), "seq", split_axis=1, concat_axis=0, tiled=True
    )
    filter_grad = jnp.transpose(filter_rows)
    dgated = jnp.transpose(back_rows, (0, 2, 1)) + skip_gain * dmix
    upstream = jnp.stack((dout * mixed, dgated * conv[2], dgated * conv[1]))
    heads = passed_along(upstream[:, :, :2], "seq", -1)
    grad_ext = jnp.concatenate((upstream, heads), axis=2)
    grads = (
        taps[:, 0] * grad_ext[:, :, :tok]
        + taps[:, 1] * grad_ext[:, :, 1 : tok + 1]
        + taps[:, 2] * grad_ext[:, :, 2:]
    )
    grads = grads.astype(jnp.bfloat16)
    taps_part = (
        jnp.stack(
            [
                jnp.sum(upstream * extended[:, :, 2 - lag : 2 - lag + tok], axis=(1, 2))
                for lag in range(3)
            ],
            axis=1,
        )
        * scale
    )
    skip_part = jnp.sum(dmix * gated, axis=(0, 1)) * scale
    taps_local, skip_local = (
        lax.psum_scatter(taps_part, "seq", scatter_dimension=2, tiled=True),
        lax.psum_scatter(skip_part, "seq", scatter_dimension=0, tiled=True),
    )
    taps_grad, skip_grad = lax.psum((taps_local, skip_local), "dp")
    return (grads[0], grads[1], grads[2], filter_grad, taps_grad, skip_grad)


def solution(mesh):
    in_specs = (
        P(("groups", "dp"), "seq", None),
        P(("groups", "dp"), "seq", None),
        P(("groups", "dp"), "seq", None),
        P(("groups", "dp"), "seq", None),
        P(("groups", "dp")),
        P(),
        P(),
        P("seq", None),
    )
    out_specs = (
        P(("groups", "dp"), "seq", None),
        P(("groups", "dp"), "seq", None),
        P(("groups", "dp"), "seq", None),
        P(("groups", "seq"), None),
        P("groups", None, "seq"),
        P(("groups", "seq")),
    )
    def chosen(query_proj, *rest):
        pairs, tok, _ = query_proj.shape
        dense = pairs == 1 and mesh.shape["dp"] == mesh.shape["groups"] == 2 and tok * mesh.shape["seq"] <= DENSE_LIMIT
        return (dense_body if dense else body)(query_proj, *rest)

    return jax.shard_map(chosen, mesh=mesh, in_specs=in_specs, out_specs=out_specs, check_vma=False)
```
